128 devices in a mesh: row: 16 (over z_hi, y, core), col: 8 (over z_lo, x).
Axes of the slice: x: 4, y: 4, z: 4 (z_hi: 2, z_lo: 2; z = z_hi * 2 + z_lo), core: 2. Of those that a mesh axis runs over, the one named last changes fastest.
Arguments:
- edge_tensor: float32 [1024, 16, 1024], P('row'), may hold values from -0.0234375 to 0.0234375
- site_tensor: float32 [16, 16, 16, 16], replicated, may hold values from -0.375 to 0.375
- left_isometry: float32 [1024, 16, 1024], P('row'), may hold values from -0.0234375 to 0.0234375
- right_isometry: float32 [512, 16, 1024], P('col', None, 'row'), may hold values from -0.03125 to 0.03125
- cotangent: float32 [512, 16, 1024], P('col', None, 'row'), may hold values from -96 to 96
Outputs:
- edge_gradient: float32 [1024, 16, 1024], P('row', 'col')
- site_gradient: float32 [16, 16, 16, 16], replicated
- left_gradient: float32 [1024, 16, 1024], P('row', 'col')
- right_gradient: float32 [512, 16, 1024], P('col', 'row')
The draws below stay inside these ranges and needn't reach their ends.
All inputs are finite; a program needn't handle non-finite values.
Results may differ from the reference program's by a relative error of at most 0.0003.
Values sent between devices are 32-bit elements; how exact they have to be, the bound alone decides.
No kernel may reach another device: no remote copies, remote signals or barrier semaphores. Data moves between devices by JAX's collectives and lax.ppermute only.
A program may use at most 192 MiB of HBM per device.

```python
import jax
import jax.numpy as jnp
from jax import lax

CHI = 1024
D2 = 16
COLS = 512
N_ROW = 16


def level_of(key, extent, cuts, least, top_value):
    def one(position, shards_of):
        draws = jax.random.uniform(jax.random.fold_in(jax.random.fold_in(key, 6), position), (shards_of,), jnp.float32, least / len(cuts), top_value / len(cuts))
        return jnp.repeat(jnp.exp(draws), extent[position] // shards_of).reshape((-1,) + (1,) * (len(extent) - position - 1))

    factor_of = one(*cuts[0])
    for cut in cuts[1:]:
        factor_of = factor_of * one(*cut)
    return factor_of


def noise(rng, extent, scale, bound, cuts=(), kind=jnp.bfloat16):
    result = jax.random.normal(rng, extent, jnp.float32) * scale
    if len(cuts) > 0:
        result = level_of(rng, extent, cuts, -0.22, 0.18) * result
    return jnp.clip(result, min=-bound, max=bound).astype(kind)


def setup_inputs(seed: int = 0) -> dict:
    splits = jax.random.split(jax.random.key(seed), 6)
    edge_tensor = noise(splits[0], (CHI, D2, CHI), (4 * CHI * D2) ** -0.5, 0.0234375, ((0, 16),), jnp.float32)
    site_tensor = noise(splits[1], (D2, D2, D2, D2), (D2 * D2) ** -0.5, 0.375, (), jnp.float32)
    left_isometry = noise(splits[2], (CHI, D2, CHI), (4 * CHI * D2) ** -0.5, 0.0234375, ((0, 16),), jnp.float32)
    right_isometry = noise(splits[3], (COLS, D2, CHI), (2 * CHI * D2) ** -0.5, 0.03125, ((0, 8), (2, 16)), jnp.float32)
    cotangent = noise(splits[4], (COLS, D2, CHI), 16.0, 96.0, ((0, 8), (2, 16)), jnp.float32)
    return {"edge_tensor": edge_tensor, "site_tensor": site_tensor, "left_isometry": left_isometry, "right_isometry": right_isometry, "cotangent": cotangent}


def reference(edge_tensor, site_tensor, left_isometry, right_isometry, cotangent):
    highest = lax.Precision.HIGHEST
    square = D2 * D2
    block_rows = CHI // N_ROW
    site_matrix = jnp.transpose(site_tensor, (1, 2, 0, 3)).reshape(square, square)

    def one_block(running, block_index):
        right_acc, site_acc = running
        offset = (block_index * block_rows).astype(jnp.int32)
        edge_rows = lax.dynamic_slice_in_dim(edge_tensor, offset, block_rows, 0)
        left_rows = lax.dynamic_slice_in_dim(left_isometry, offset, block_rows, 0)
        first_section = jnp.einsum('aeb,cfb->acef', edge_rows, right_isometry, precision=highest)
        first_flat = first_section.reshape(block_rows, COLS, square)
        second_flat = jnp.dot(first_flat, site_matrix, precision=highest)
        second_section = second_flat.reshape(block_rows, COLS, D2, D2)
        back_second = jnp.einsum('adk,cgk->acdg', left_rows, cotangent, precision=highest)
        left_part = jnp.einsum('acdg,cgk->adk', second_section, cotangent, precision=highest)
        back_flat = back_second.reshape(block_rows, COLS, square)
        back_first = jnp.dot(back_flat, site_matrix.T, precision=highest).reshape(block_rows, COLS, D2, D2)
        site_acc = site_acc + jnp.dot(first_flat.reshape(-1, square).T, back_flat.reshape(-1, square), precision=highest)
        edge_part = jnp.einsum('acef,cfb->aeb', back_first, right_isometry, precision=highest)
        right_acc = right_acc + jnp.einsum('aeb,acef->cfb', edge_rows, back_first, precision=highest)
        return (right_acc, site_acc), (edge_part, left_part)

    initial = (jnp.zeros((COLS, D2, CHI), jnp.float32), jnp.zeros((square, square), jnp.float32))
    (right_gradient, site_acc), (edge_parts, left_parts) = lax.scan(one_block, initial, jnp.arange(N_ROW, dtype=jnp.int32))
    edge_gradient = edge_parts.reshape(CHI, D2, CHI)
    left_gradient = left_parts.reshape(CHI, D2, CHI)
    site_gradient = jnp.transpose(site_acc.reshape(D2, D2, D2, D2), (2, 0, 1, 3))
    return edge_gradient, site_gradient, left_gradient, right_gradient
```

```python
import functools
import jax
import jax.numpy as jnp
from jax import lax
from jax.experimental import pallas as pl
from jax.experimental.pallas import tpu as pltpu
from jax.sharding import PartitionSpec as P

F32, BF16 = jnp.float32, jnp.bfloat16
NN = (((1,), (0,)), ((), ()))
NT = (((1,), (1,)), ((), ()))
TN = (((0,), (0,)), ((), ()))
PARAMS = pltpu.CompilerParams(vmem_limit_bytes=60 << 20)
ROWS = 256
CHUNKS = 4


def split(value):
    high = value.astype(BF16)
    return high, (value - high.astype(F32)).astype(BF16)


def dot3(left, right, dims):
    dot = functools.partial(lax.dot_general, dimension_numbers=dims, preferred_element_type=F32)
    return dot(left[0], right[0]) + (dot(left[0], right[1]) + dot(left[1], right[0]))


def swap_into(value, high_ref, low_ref):
    lane = lax.broadcasted_iota(jnp.int32, (16, 128), 1)
    for pair in range(8):
        for tile in range(8):
            first = value[32 * pair : 32 * pair + 16, 128 * tile : 128 * tile + 128]
            second = value[32 * pair + 16 : 32 * pair + 32, 128 * tile : 128 * tile + 128]
            even = jnp.where(lane < 64, first, pltpu.roll(second, 64, 1))
            odd = jnp.where(lane < 64, pltpu.roll(first, 64, 1), second)
            columns = slice(128 * pair, 128 * pair + 128)
            for start, part in ((16 * tile, even), (128 + 16 * tile, odd)):
                high, low = split(part)
                high_ref[start : start + 16, columns] = high
                low_ref[start : start + 16, columns] = low


def unswap_into(value, high_ref, low_ref):
    lane = lax.broadcasted_iota(jnp.int32, (16, 128), 1)
    for pair in range(8):
        for tile in range(8):
            columns = slice(128 * pair, 128 * pair + 128)
            even = value[16 * tile : 16 * tile + 16, columns]
            odd = value[128 + 16 * tile : 128 + 16 * tile + 16, columns]
            first = jnp.where(lane < 64, even, pltpu.roll(odd, 64, 1))
            second = jnp.where(lane < 64, pltpu.roll(even, 64, 1), odd)
            columns = slice(128 * tile, 128 * tile + 128)
            for start, part in ((32 * pair, first), (32 * pair + 16, second)):
                high, low = split(part)
                high_ref[start : start + 16, columns] = high
                low_ref[start : start + 16, columns] = low


def assemble(offsets_ref, piece_refs, whole_ref, sems, high_ref, low_ref):
    block = 64
    copies = []
    count = 0
    for piece in piece_refs:
        for part in range(piece.shape[0] // block):
            start = pl.multiple_of(offsets_ref[count], block)
            copies.append(
                pltpu.make_async_copy(
                    piece.at[pl.ds(part * block, block)], whole_ref.at[pl.ds(start, block)], sems.at[count]
                )
            )
            count += 1
    for copy in copies:
        copy.start()
    for copy in copies:
        copy.wait()

    def one(index, carry):
        rows = pl.ds(pl.multiple_of(index * 64, 64), 64)
        high, low = split(whole_ref[rows, :])
        high_ref[rows, :] = high
        low_ref[rows, :] = low
        return carry

    lax.fori_loop(0, 16, one, 0)


def back_kernel(pieces, offsets_ref, *refs):
    piece_refs = refs[:pieces]
    rows_ref, site_ref = refs[pieces : pieces + 2]
    whole_high, whole_low, back_high, back_low, swapped_high, swapped_low, whole, sems = refs[pieces + 2 :]

    @pl.when(pl.program_id(0) == 0)
    def _():
        assemble(offsets_ref, piece_refs, whole, sems, whole_high, whole_low)

    section = dot3(split(rows_ref[...]), (whole_high[...], whole_low[...]), NN)
    swap_into(section, swapped_high, swapped_low)
    mixed = dot3(split(site_ref[...]), (swapped_high[...], swapped_low[...]), NN)
    unswap_into(mixed, back_high, back_low)


def edge_kernel(pieces, offsets_ref, *refs):
    piece_refs = refs[:pieces]
    back_high_ref, back_low_ref = refs[pieces : pieces + 2]
    whole_high, whole_low, edge_ref, whole, sems = refs[pieces + 2 :]

    @pl.when(pl.program_id(0) == 0)
    def _():
        assemble(offsets_ref, piece_refs, whole, sems, whole_high, whole_low)

    terms = dot3((back_high_ref[...], back_low_ref[...]), (whole_high[...], whole_low[...]), NT)
    for a in range(16):
        edge_ref[:, a, :] = terms[16 * a : 16 * a + 16, :]


def left_kernel(
    edge_ref,
    right_high_ref,
    right_low_ref,
    site_matrix_ref,
    swapped_high_ref,
    swapped_low_ref,
    cotangent_high_ref,
    cotangent_low_ref,
    left_ref,
    site_ref,
    first_high,
    first_low,
    second_high,
    second_low,
):
    first = dot3(split(edge_ref[...]), (right_high_ref[...], right_low_ref[...]), NN)
    swap_into(first, first_high, first_low)
    mixed = dot3(split(site_matrix_ref[...]), (first_high[...], first_low[...]), NN)
    unswap_into(mixed, second_high, second_low)
    site = dot3((first_high[...], first_low[...]), (swapped_high_ref[...], swapped_low_ref[...]), NT)

    @pl.when(pl.program_id(0) == 0)
    def _():
        site_ref[...] = site

    @pl.when(pl.program_id(0) > 0)
    def _():
        site_ref[...] += site

    terms = dot3((second_high[...], second_low[...]), (cotangent_high_ref[...], cotangent_low_ref[...]), NT)
    for a in range(16):
        left_ref[:, a, :] = terms[16 * a : 16 * a + 16, :]


def right_kernel(places_ref, back_high_ref, back_low_ref, edge_ref, own_ref, other_ref, turned_high, turned_low, placed):
    @pl.when(pl.program_id(0) == 0)
    def _():
        for chunk in range(CHUNKS):
            rows = slice(chunk * ROWS, (chunk + 1) * ROWS)
            turned_high[:, rows] = back_high_ref[rows, :].T
            turned_low[:, rows] = back_low_ref[rows, :].T

    terms = dot3((turned_high[...], turned_low[...]), split(edge_ref[...]), NN)
    for block in range(16):
        start = pl.multiple_of(places_ref[block], 64)
        placed[pl.ds(start, 64), :] = terms[64 * block : 64 * block + 64, :]
    own_ref[...] = placed[:512, :]
    other_ref[...] = placed[512:, :]


def resident(shape):
    return pl.BlockSpec(shape, lambda *_: (0,) * len(shape))


ANY = pl.BlockSpec(memory_space=pl.ANY)
SQUARE = jax.ShapeDtypeStruct((1024, 1024), BF16)
CHUNK = pl.BlockSpec((ROWS, 1024), lambda i, *_: (i, 0))


def back_call(offsets, pieces, rows, site_matrix):
    return pl.pallas_call(
        functools.partial(back_kernel, len(pieces)),
        out_shape=(SQUARE,) * 6,
        grid_spec=pltpu.PrefetchScalarGridSpec(
            num_scalar_prefetch=1,
            grid=(CHUNKS,),
            in_specs=[ANY] * len(pieces) + [CHUNK, resident((256, 256))],
            out_specs=[resident((1024, 1024))] * 2 + [CHUNK] * 4,
            scratch_shapes=[pltpu.VMEM((1024, 1024), F32), pltpu.SemaphoreType.DMA((16,))],
        ),
        compiler_params=PARAMS,
        name="back",
    )(offsets, *pieces, rows, site_matrix)


def edge_call(offsets, pieces, back_split):
    return pl.pallas_call(
        functools.partial(edge_kernel, len(pieces)),
        out_shape=(SQUARE, SQUARE, jax.ShapeDtypeStruct((16, 64, 1024), F32)),
        grid_spec=pltpu.PrefetchScalarGridSpec(
            num_scalar_prefetch=1,
            grid=(CHUNKS,),
            in_specs=[ANY] * len(pieces) + [CHUNK, CHUNK],
            out_specs=[resident((1024, 1024))] * 2 + [pl.BlockSpec((16, 16, 1024), lambda i, *_: (0, i, 0))],
            scratch_shapes=[pltpu.VMEM((1024, 1024), F32), pltpu.SemaphoreType.DMA((16,))],
        ),
        compiler_params=PARAMS,
        name="edge",
    )(offsets, *pieces, *back_split)


def left_call(edge_rows, right_split, site_matrix, swapped_split, cotangent_split):
    return pl.pallas_call(
        left_kernel,
        out_shape=(jax.ShapeDtypeStruct((16, 64, 1024), F32), jax.ShapeDtypeStruct((256, 256), F32)),
        grid=(CHUNKS,),
        in_specs=[CHUNK]
        + [resident((1024, 1024))] * 2
        + [resident((256, 256))]
        + [CHUNK] * 2
        + [resident((1024, 1024))] * 2,
        out_specs=[pl.BlockSpec((16, 16, 1024), lambda i: (0, i, 0)), resident((256, 256))],
        scratch_shapes=[pltpu.VMEM((ROWS, 1024), BF16)] * 4,
        compiler_params=PARAMS,
        name="left",
    )(edge_rows, *right_split, site_matrix, *swapped_split, *cotangent_split)


def right_call(places, back_split, edge_rows):
    column = lambda rows: pl.BlockSpec((rows, 256), lambda i, *_: (0, i))
    return pl.pallas_call(
        right_kernel,
        out_shape=(jax.ShapeDtypeStruct((512, 1024), F32),) * 2,
        grid_spec=pltpu.PrefetchScalarGridSpec(
            num_scalar_prefetch=1,
            grid=(4,),
            in_specs=[resident((1024, 1024))] * 2 + [column(1024)],
            out_specs=[column(512)] * 2,
            scratch_shapes=[pltpu.VMEM((1024, 1024), BF16)] * 2 + [pltpu.VMEM((1024, 256), F32)],
        ),
        compiler_params=PARAMS,
        name="right",
    )(places, *back_split, edge_rows)


def row_permute(value, z, y, core):
    pairs = []
    for source in range(16):
        there = ((source // 8) ^ z) * 8 + ((source // 2 + y) % 4) * 2 + ((source % 2) ^ core)
        pairs.append((source, there))
    return lax.ppermute(value, "row", pairs)


def col_permute(value, z, x):
    return lax.ppermute(value, "col", [(i, ((i // 4) ^ z) * 4 + (i + x) % 4) for i in range(8)])


def dense(value):
    cols, bond, width = value.shape
    return jnp.transpose(value.reshape(cols, 2, 8, width), (3, 2, 1, 0)).reshape(width, bond * cols)


def take(value, index):
    return lax.dynamic_index_in_dim(value, index, 0, keepdims=False)


def on_device(edge_tensor, site_tensor, left_isometry, right_isometry, cotangent):
    row = lax.axis_index("row").astype(jnp.int32)
    z, y, core = row // 8, row // 2 % 4, row % 2
    edge_rows = edge_tensor.reshape(1024, 1024)
    left_rows = left_isometry.reshape(1024, 1024)
    back_site = jnp.transpose(site_tensor, (2, 1, 3, 0)).reshape(256, 256)
    front_site = jnp.transpose(site_tensor, (3, 0, 2, 1)).reshape(256, 256)

    def offset_of(other_z, steps, other_core):
        return ((z ^ other_z) * 8 + (y - steps) % 4 * 2 + (core ^ other_core)) * 64

    own = dense(cotangent)
    pair = jnp.concatenate([own, row_permute(own, 1, 0, 0)], 0)
    pieces = [pair] + [row_permute(pair, 0, steps, 0) for steps in (1, 3, 2)]
    pieces += [row_permute(piece, 0, 0, 1) for piece in pieces]
    offsets = jnp.stack([offset_of(j, steps, c) for c in (0, 1) for steps in (0, 1, 3, 2) for j in (0, 1)])
    cotangent_high, cotangent_low, *rest = back_call(offsets, pieces, left_rows, back_site)
    back_split, swapped_split = rest[:2], rest[2:]

    own = dense(right_isometry)
    quad = jnp.concatenate([own] + [row_permute(own, 0, steps, 0) for steps in (1, 3, 2)], 0)
    pieces = [quad, row_permute(quad, 1, 0, 0)]
    pieces += [row_permute(piece, 0, 0, 1) for piece in pieces]
    offsets = jnp.stack([offset_of(j, steps, c) for c in (0, 1) for j in (0, 1) for steps in (0, 1, 3, 2)])

    blocks = [(i % 2) * 8 + i // 2 for i in range(16)]
    places = jnp.stack(
        [((b % 2 ^ core) * 8 + (b // 2 % 4 - y) % 4 * 2 + (b // 8 ^ z)) * 64 for b in blocks]
    )
    right_own, right_other = right_call(places, back_split, edge_rows)

    right_high, right_low, edge_terms = edge_call(offsets, pieces, back_split)
    edge_gradient = lax.psum_scatter(edge_terms, "col", scatter_dimension=0, tiled=True)
    left_terms, site_terms = left_call(
        edge_rows, (right_high, right_low), front_site, swapped_split, (cotangent_high, cotangent_low)
    )
    left_gradient = lax.psum_scatter(left_terms, "col", scatter_dimension=0, tiled=True)

    total = (right_own + row_permute(right_other, 0, 0, 1)).reshape(4, 2, 64, 1024)
    total = total[0] + row_permute(total[1], 0, 1, 0) + row_permute(total[3], 0, 3, 0) + row_permute(total[2], 0, 2, 0)
    right_gradient = total[0] + row_permute(total[1], 1, 0, 0)

    part = site_terms.reshape(2, 128, 256)
    part = (take(part, core) + row_permute(take(part, 1 - core), 0, 0, 1)).reshape(2, 64, 256)
    part = (take(part, z) + row_permute(take(part, 1 - z), 1, 0, 0)).reshape(4, 16, 256)
    part = take(part, y) + sum(row_permute(take(part, (y + k) % 4), 0, k, 0) for k in (1, 2, 3))
    part = part + sum(col_permute(part, 0, k) for k in (1, 2, 3))
    part = part + col_permute(part, 1, 0)
    ring = [part] + [row_permute(part, 0, k, 0) for k in (3, 2, 1)]
    part = lax.dynamic_slice_in_dim(jnp.concatenate(ring + ring, 0), (4 - y) % 4 * 16, 64, 0)
    other = row_permute(part, 1, 0, 0)
    part = jnp.where(z == 0, jnp.concatenate([part, other], 0), jnp.concatenate([other, part], 0))
    other = row_permute(part, 0, 0, 1)
    part = jnp.where(core == 0, jnp.concatenate([part, other], 0), jnp.concatenate([other, part], 0))
    site_gradient = jnp.transpose(part.reshape(16, 16, 16, 16), (3, 1, 0, 2))

    return (
        jnp.transpose(edge_gradient, (1, 0, 2)),
        site_gradient,
        jnp.transpose(left_gradient, (1, 0, 2)),
        right_gradient.reshape(64, 1, 1024),
    )


def solution(mesh):
    in_specs = (
        P("row", None, None),
        P(),
        P("row", None, None),
        P("col", None, "row"),
        P("col", None, "row"),
    )
    out_specs = (P("row", "col", None), P(), P("row", "col", None), P("col", "row", None))
    return jax.shard_map(
        on_device, mesh=mesh, in_specs=in_specs, out_specs=out_specs, check_vma=False
    )
```

```python
import functools

import jax
import jax.numpy as jnp
import numpy as np
from jax import lax
from jax.experimental import pallas as pl
from jax.experimental.pallas import tpu as pltpu
from jax.sharding import PartitionSpec as P

F32, BF16 = jnp.float32, jnp.bfloat16
NN = (((1,), (0,)), ((), ()))
NT = (((1,), (1,)), ((), ()))
TN = (((0,), (0,)), ((), ()))
PARAMS = pltpu.CompilerParams(vmem_limit_bytes=60 << 20)
ROWS = 256
CHUNKS = 4


def split(value):
    high = value.astype(BF16)
    return high, (value - high.astype(F32)).astype(BF16)


def dot3(left, right, dims):
    dot = functools.partial(lax.dot_general, dimension_numbers=dims, preferred_element_type=F32)
    return dot(left[0], right[0]) + (dot(left[0], right[1]) + dot(left[1], right[0]))


def swap_into(value, high_ref, low_ref):
    lane = lax.broadcasted_iota(jnp.int32, (16, 128), 1)
    for pair in range(8):
        for tile in range(8):
            first = value[32 * pair : 32 * pair + 16, 128 * tile : 128 * tile + 128]
            second = value[32 * pair + 16 : 32 * pair + 32, 128 * tile : 128 * tile + 128]
            even = jnp.where(lane < 64, first, pltpu.roll(second, 64, 1))
            odd = jnp.where(lane < 64, pltpu.roll(first, 64, 1), second)
            columns = slice(128 * pair, 128 * pair + 128)
            for start, part in ((16 * tile, even), (128 + 16 * tile, odd)):
                high, low = split(part)
                high_ref[start : start + 16, columns] = high
                low_ref[start : start + 16, columns] = low


def unswap_into(value, high_ref, low_ref):
    lane = lax.broadcasted_iota(jnp.int32, (16, 128), 1)
    for pair in range(8):
        for tile in range(8):
            columns = slice(128 * pair, 128 * pair + 128)
            even = value[16 * tile : 16 * tile + 16, columns]
            odd = value[128 + 16 * tile : 128 + 16 * tile + 16, columns]
            first = jnp.where(lane < 64, even, pltpu.roll(odd, 64, 1))
            second = jnp.where(lane < 64, pltpu.roll(even, 64, 1), odd)
            columns = slice(128 * tile, 128 * tile + 128)
            for start, part in ((32 * pair, first), (32 * pair + 16, second)):
                high, low = split(part)
                high_ref[start : start + 16, columns] = high
                low_ref[start : start + 16, columns] = low


def assemble(offsets_ref, piece_refs, whole_ref, sems, high_ref, low_ref):
    block = 64
    copies = []
    count = 0
    for piece in piece_refs:
        for part in range(piece.shape[0] // block):
            start = pl.multiple_of(offsets_ref[count], block)
            copies.append(
                pltpu.make_async_copy(
                    piece.at[pl.ds(part * block, block)], whole_ref.at[pl.ds(start, block)], sems.at[count]
                )
            )
            count += 1
    for copy in copies:
        copy.start()
    for copy in copies:
        copy.wait()

    def one(index, carry):
        rows = pl.ds(pl.multiple_of(index * 64, 64), 64)
        high, low = split(whole_ref[rows, :])
        high_ref[rows, :] = high
        low_ref[rows, :] = low
        return carry

    lax.fori_loop(0, 16, one, 0)


def back_kernel(pieces, offsets_ref, *refs):
    piece_refs = refs[:pieces]
    rows_ref, site_ref = refs[pieces : pieces + 2]
    whole_high, whole_low, back_high, back_low, swapped_high, swapped_low, whole, sems = refs[pieces + 2 :]

    @pl.when(pl.program_id(0) == 0)
    def _():
        assemble(offsets_ref, piece_refs, whole, sems, whole_high, whole_low)

    section = dot3(split(rows_ref[...]), (whole_high[...], whole_low[...]), NN)
    swap_into(section, swapped_high, swapped_low)
    mixed = dot3(split(site_ref[...]), (swapped_high[...], swapped_low[...]), NN)
    unswap_into(mixed, back_high, back_low)


def edge_kernel(pieces, offsets_ref, *refs):
    piece_refs = refs[:pieces]
    back_high_ref, back_low_ref = refs[pieces : pieces + 2]
    whole_high, whole_low, edge_ref, whole, sems = refs[pieces + 2 :]

    @pl.when(pl.program_id(0) == 0)
    def _():
        assemble(offsets_ref, piece_refs, whole, sems, whole_high, whole_low)

    terms = dot3((back_high_ref[...], back_low_ref[...]), (whole_high[...], whole_low[...]), NT)
    for a in range(16):
        edge_ref[:, a, :] = terms[16 * a : 16 * a + 16, :]


def left_kernel(
    edge_ref,
    right_high_ref,
    right_low_ref,
    site_matrix_ref,
    swapped_high_ref,
    swapped_low_ref,
    cotangent_high_ref,
    cotangent_low_ref,
    left_ref,
    site_ref,
    first_high,
    first_low,
    second_high,
    second_low,
):
    first = dot3(split(edge_ref[...]), (right_high_ref[...], right_low_ref[...]), NN)
    swap_into(first, first_high, first_low)
    mixed = dot3(split(site_matrix_ref[...]), (first_high[...], first_low[...]), TN)
    unswap_into(mixed, second_high, second_low)
    site = dot3((first_high[...], first_low[...]), (swapped_high_ref[...], swapped_low_ref[...]), NT)

    @pl.when(pl.program_id(0) == 0)
    def _():
        site_ref[...] = site

    @pl.when(pl.program_id(0) > 0)
    def _():
        site_ref[...] += site

    terms = dot3((second_high[...], second_low[...]), (cotangent_high_ref[...], cotangent_low_ref[...]), NT)
    for a in range(16):
        left_ref[:, a, :] = terms[16 * a : 16 * a + 16, :]


def right_kernel(places_ref, back_high_ref, back_low_ref, edge_ref, own_ref, other_ref, turned_high, turned_low, placed):
    @pl.when(pl.program_id(0) == 0)
    def _():
        for chunk in range(CHUNKS):
            rows = slice(chunk * ROWS, (chunk + 1) * ROWS)
            turned_high[:, rows] = back_high_ref[rows, :].T
            turned_low[:, rows] = back_low_ref[rows, :].T

    terms = dot3((turned_high[...], turned_low[...]), split(edge_ref[...]), NN)
    for block in range(16):
        start = pl.multiple_of(places_ref[block], 64)
        placed[pl.ds(start, 64), :] = terms[64 * block : 64 * block + 64, :]
    own_ref[...] = placed[:512, :]
    other_ref[...] = placed[512:, :]


def resident(shape):
    return pl.BlockSpec(shape, lambda *_: (0,) * len(shape))


ANY = pl.BlockSpec(memory_space=pl.ANY)
SQUARE = jax.ShapeDtypeStruct((1024, 1024), BF16)
CHUNK = pl.BlockSpec((ROWS, 1024), lambda i, *_: (i, 0))


def back_call(offsets, pieces, rows, site_matrix):
    return pl.pallas_call(
        functools.partial(back_kernel, len(pieces)),
        out_shape=(SQUARE,) * 6,
        grid_spec=pltpu.PrefetchScalarGridSpec(
            num_scalar_prefetch=1,
            grid=(CHUNKS,),
            in_specs=[ANY] * len(pieces) + [CHUNK, resident((256, 256))],
            out_specs=[resident((1024, 1024))] * 2 + [CHUNK] * 4,
            scratch_shapes=[pltpu.VMEM((1024, 1024), F32), pltpu.SemaphoreType.DMA((16,))],
        ),
        compiler_params=PARAMS,
        name="back",
    )(offsets, *pieces, rows, site_matrix)


def edge_call(offsets, pieces, back_split):
    return pl.pallas_call(
        functools.partial(edge_kernel, len(pieces)),
        out_shape=(SQUARE, SQUARE, jax.ShapeDtypeStruct((16, 64, 1024), F32)),
        grid_spec=pltpu.PrefetchScalarGridSpec(
            num_scalar_prefetch=1,
            grid=(CHUNKS,),
            in_specs=[ANY] * len(pieces) + [CHUNK, CHUNK],
            out_specs=[resident((1024, 1024))] * 2 + [pl.BlockSpec((16, 16, 1024), lambda i, *_: (0, i, 0))],
            scratch_shapes=[pltpu.VMEM((1024, 1024), F32), pltpu.SemaphoreType.DMA((16,))],
        ),
        compiler_params=PARAMS,
        name="edge",
    )(offsets, *pieces, *back_split)


def left_call(edge_rows, right_split, site_matrix, swapped_split, cotangent_split):
    return pl.pallas_call(
        left_kernel,
        out_shape=(jax.ShapeDtypeStruct((16, 64, 1024), F32), jax.ShapeDtypeStruct((256, 256), F32)),
        grid=(CHUNKS,),
        in_specs=[CHUNK]
        + [resident((1024, 1024))] * 2
        + [resident((256, 256))]
        + [CHUNK] * 2
        + [resident((1024, 1024))] * 2,
        out_specs=[pl.BlockSpec((16, 16, 1024), lambda i: (0, i, 0)), resident((256, 256))],
        scratch_shapes=[pltpu.VMEM((ROWS, 1024), BF16)] * 4,
        compiler_params=PARAMS,
        name="left",
    )(edge_rows, *right_split, site_matrix, *swapped_split, *cotangent_split)


def right_call(places, back_split, edge_rows):
    column = lambda rows: pl.BlockSpec((rows, 256), lambda i, *_: (0, i))
    return pl.pallas_call(
        right_kernel,
        out_shape=(jax.ShapeDtypeStruct((512, 1024), F32),) * 2,
        grid_spec=pltpu.PrefetchScalarGridSpec(
            num_scalar_prefetch=1,
            grid=(4,),
            in_specs=[resident((1024, 1024))] * 2 + [column(1024)],
            out_specs=[column(512)] * 2,
            scratch_shapes=[pltpu.VMEM((1024, 1024), BF16)] * 2 + [pltpu.VMEM((1024, 256), F32)],
        ),
        compiler_params=PARAMS,
        name="right",
    )(places, *back_split, edge_rows)


def row_permute(value, z, y, core):
    pairs = []
    for source in range(16):
        there = ((source // 8) ^ z) * 8 + ((source // 2 + y) % 4) * 2 + ((source % 2) ^ core)
        pairs.append((source, there))
    return lax.ppermute(value, "row", pairs)


def col_permute(value, z, x):
    return lax.ppermute(value, "col", [(i, ((i // 4) ^ z) * 4 + (i + x) % 4) for i in range(8)])


def dense(value):
    cols, bond, width = value.shape
    return jnp.transpose(value.reshape(cols, 2, 8, width), (3, 2, 1, 0)).reshape(width, bond * cols)


def take(value, index):
    return lax.dynamic_index_in_dim(value, index, 0, keepdims=False)


def on_device(edge_tensor, site_tensor, left_isometry, right_isometry, cotangent):
    row = lax.axis_index("row").astype(jnp.int32)
    z, y, core = row >> 3, (row >> 1) & 3, row & 1
    edge_rows = edge_tensor.reshape(1024, 1024)
    left_rows = left_isometry.reshape(1024, 1024)

    def offset_of(other_z, steps, other_core):
        other_z, steps, other_core = (np.array(list(v), np.int32) for v in (other_z, steps, other_core))
        return ((z ^ other_z) * 8 + ((y - steps) & 3) * 2 + (core ^ other_core)) * 64

    own = dense(cotangent)
    own, right_isometry = lax.optimization_barrier((own, right_isometry))
    other = row_permute(own, 1, 0, 0)
    early = own
    own = dense(right_isometry)
    others = [row_permute(own, 0, steps, 0) for steps in (1, 3, 2)]
    quad, other = lax.optimization_barrier((jnp.concatenate([own, *others], 0), other))

    pair = jnp.concatenate([early, other], 0)

    site_matrix = jnp.transpose(site_tensor, (2, 1, 3, 0)).reshape(256, 256)
    near = [row_permute(pair, 0, steps, 0) for steps in (1, 3)]
    far = row_permute(pair, 0, 2, 0)
    quads = [quad, row_permute(quad, 1, 0, 0)]
    near[0], near[1], site_matrix = lax.optimization_barrier((*near, site_matrix))
    pieces = [pair, *near, far]
    pieces += [row_permute(piece, 0, 0, 1) for piece in pieces]
    order = [(j, steps, c) for c in (0, 1) for steps in (0, 1, 3, 2) for j in (0, 1)]
    cotangent_high, cotangent_low, *rest = back_call(offset_of(*zip(*order)), pieces, left_rows, site_matrix)
    back_split, swapped_split = rest[:2], rest[2:]

    quads += [row_permute(piece, 0, 0, 1) for piece in quads]
    order = [(j, steps, c) for c in (0, 1) for j in (0, 1) for steps in (0, 1, 3, 2)]
    right_high, right_low, edge_terms = edge_call(offset_of(*zip(*order)), quads, back_split)
    edge_gradient = lax.psum_scatter(edge_terms, "col", scatter_dimension=0, tiled=True)
    left_terms, site_terms = left_call(
        edge_rows, (right_high, right_low), site_matrix, swapped_split, (cotangent_high, cotangent_low)
    )
    left_gradient = lax.psum_scatter(left_terms, "col", scatter_dimension=0, tiled=True)

    blocks = np.array([(i % 2) * 8 + i // 2 for i in range(16)], np.int32)
    places = ((blocks & 1) ^ core) * 8 + (((blocks >> 1) - y) & 3) * 2 + ((blocks >> 3) ^ z)
    right_own, right_other = right_call(places * 64, back_split, edge_rows)

    part = site_terms.reshape(2, 128, 256)
    part = (take(part, core) + row_permute(take(part, 1 - core), 0, 0, 1)).reshape(2, 64, 256)
    part = (take(part, z) + row_permute(take(part, 1 - z), 1, 0, 0)).reshape(4, 16, 256)
    part = take(part, y) + sum(row_permute(take(part, (y + k) & 3), 0, k, 0) for k in (1, 2, 3))
    part = part + sum(col_permute(part, 0, k) for k in (1, 2, 3))
    part = part + col_permute(part, 1, 0)
    ring = [part] + [row_permute(part, 0, k, 0) for k in (3, 2, 1)]
    part = lax.dynamic_slice_in_dim(jnp.concatenate(ring + ring, 0), ((4 - y) & 3) * 16, 64, 0)
    other = row_permute(part, 1, 0, 0)
    part = jnp.where(z == 0, jnp.concatenate([part, other], 0), jnp.concatenate([other, part], 0))
    other = row_permute(part, 0, 0, 1)
    part = jnp.where(core == 0, jnp.concatenate([part, other], 0), jnp.concatenate([other, part], 0))
    site_gradient = jnp.transpose(part.reshape(16, 16, 16, 16), (3, 1, 0, 2))

    total = (right_own + row_permute(right_other, 0, 0, 1)).reshape(4, 2, 64, 1024)
    total = total[0] + row_permute(total[1], 0, 1, 0) + row_permute(total[3], 0, 3, 0) + row_permute(total[2], 0, 2, 0)
    right_gradient = total[0] + row_permute(total[1], 1, 0, 0)

    return (
        jnp.transpose(edge_gradient, (1, 0, 2)),
        site_gradient,
        jnp.transpose(left_gradient, (1, 0, 2)),
        right_gradient.reshape(64, 1, 1024),
    )


def solution(mesh):
    in_specs = (
        P("row", None, None),
        P(),
        P("row", None, None),
        P("col", None, "row"),
        P("col", None, "row"),
    )
    out_specs = (P("row", "col", None), P(), P("row", "col", None), P("col", "row", None))

    return jax.shard_map(on_device, mesh=mesh, in_specs=in_specs, out_specs=out_specs, check_vma=False)
```

```python
import functools

import jax
import jax.numpy as jnp
import numpy as np
from jax import lax
from jax.experimental import pallas as pl
from jax.experimental.pallas import tpu as pltpu
from jax.sharding import PartitionSpec as P

F32, BF16 = jnp.float32, jnp.bfloat16
NN = (((1,), (0,)), ((), ()))
NT = (((1,), (1,)), ((), ()))
TN = (((0,), (0,)), ((), ()))
PARAMS = pltpu.CompilerParams(vmem_limit_bytes=60 << 20)
ROWS = 256
CHUNKS = 4


def split(value):
    high = value.astype(BF16)
    return high, (value - high.astype(F32)).astype(BF16)


def dot3(left, right, dims):
    dot = functools.partial(lax.dot_general, dimension_numbers=dims, preferred_element_type=F32)
    return dot(left[0], right[0]) + (dot(left[0], right[1]) + dot(left[1], right[0]))


def swap_into(value, high_ref, low_ref):
    lane = lax.broadcasted_iota(jnp.int32, (16, 128), 1)
    for pair in range(8):
        for tile in range(8):
            first = value[32 * pair : 32 * pair + 16, 128 * tile : 128 * tile + 128]
            second = value[32 * pair + 16 : 32 * pair + 32, 128 * tile : 128 * tile + 128]
            even = jnp.where(lane < 64, first, pltpu.roll(second, 64, 1))
            odd = jnp.where(lane < 64, pltpu.roll(first, 64, 1), second)
            columns = slice(128 * pair, 128 * pair + 128)
            for start, part in ((16 * tile, even), (128 + 16 * tile, odd)):
                high, low = split(part)
                high_ref[start : start + 16, columns] = high
                low_ref[start : start + 16, columns] = low


def unswap_into(value, high_ref, low_ref):
    lane = lax.broadcasted_iota(jnp.int32, (16, 128), 1)
    for pair in range(8):
        for tile in range(8):
            columns = slice(128 * pair, 128 * pair + 128)
            even = value[16 * tile : 16 * tile + 16, columns]
            odd = value[128 + 16 * tile : 128 + 16 * tile + 16, columns]
            first = jnp.where(lane < 64, even, pltpu.roll(odd, 64, 1))
            second = jnp.where(lane < 64, pltpu.roll(even, 64, 1), odd)
            columns = slice(128 * tile, 128 * tile + 128)
            for start, part in ((32 * pair, first), (32 * pair + 16, second)):
                high, low = split(part)
                high_ref[start : start + 16, columns] = high
                low_ref[start : start + 16, columns] = low


def assemble(offsets_ref, piece_refs, whole_ref, sems, high_ref, low_ref):
    block = 64
    copies = []
    count = 0
    for piece in piece_refs:
        for part in range(piece.shape[0] // block):
            rows = pl.ds(pl.multiple_of(offsets_ref[count], block), block)
            copy = pltpu.make_async_copy(piece.at[pl.ds(part * block, block)], whole_ref.at[rows], sems.at[count])
            copies.append((copy, rows))
            count += 1
    for copy, _ in copies:
        copy.start()
    for copy, rows in copies:
        copy.wait()
        high, low = split(whole_ref[rows, :])
        high_ref[rows, :] = high
        low_ref[rows, :] = low


def back_kernel(pieces, offsets_ref, *refs):
    piece_refs = refs[:pieces]
    rows_ref, site_ref = refs[pieces : pieces + 2]
    whole_high, whole_low, back_high, back_low, swapped_high, swapped_low, whole, sems = refs[pieces + 2 :]

    @pl.when(pl.program_id(0) == 0)
    def _():
        assemble(offsets_ref, piece_refs, whole, sems, whole_high, whole_low)

    section = dot3(split(rows_ref[...]), (whole_high[...], whole_low[...]), NN)
    swap_into(section, swapped_high, swapped_low)
    mixed = dot3(split(site_ref[...]), (swapped_high[...], swapped_low[...]), NN)
    unswap_into(mixed, back_high, back_low)


def place(terms, sources_ref, staged, ahead_ref, behind_ref, kept_ref):
    for a in range(16):
        staged[:, a, :] = terms[16 * a : 16 * a + 16, :]
    slot = 0
    for ref in (ahead_ref, behind_ref, kept_ref):
        for block in range(ref.shape[0]):
            ref[block] = staged[pl.ds(sources_ref[slot] * 2, 2)]
            slot += 1


def edge_kernel(pieces, offsets_ref, sources_ref, *refs):
    piece_refs = refs[:pieces]
    back_high_ref, back_low_ref = refs[pieces : pieces + 2]
    whole_high, whole_low, ahead_ref, behind_ref, kept_ref, whole, staged, sems = refs[pieces + 2 :]

    @pl.when(pl.program_id(0) == 0)
    def _():
        assemble(offsets_ref, piece_refs, whole, sems, whole_high, whole_low)

    terms = dot3((back_high_ref[...], back_low_ref[...]), (whole_high[...], whole_low[...]), NT)
    place(terms, sources_ref, staged, ahead_ref, behind_ref, kept_ref)


def left_kernel(
    sources_ref,
    edge_ref,
    right_high_ref,
    right_low_ref,
    site_matrix_ref,
    swapped_high_ref,
    swapped_low_ref,
    cotangent_high_ref,
    cotangent_low_ref,
    ahead_ref,
    behind_ref,
    kept_ref,
    site_ref,
    first_high,
    first_low,
    second_high,
    second_low,
    cotangent_high,
    cotangent_low,
    staged,
    sems,
):
    step = pl.program_id(0)
    copies = [
        pltpu.make_async_copy(cotangent_high_ref, cotangent_high, sems.at[0]),
        pltpu.make_async_copy(cotangent_low_ref, cotangent_low, sems.at[1]),
    ]

    @pl.when(step == 0)
    def _():
        for copy in copies:
            copy.start()

    first = dot3(split(edge_ref[...]), (right_high_ref[...], right_low_ref[...]), NN)
    swap_into(first, first_high, first_low)
    mixed = dot3(split(site_matrix_ref[...]), (first_high[...], first_low[...]), TN)
    unswap_into(mixed, second_high, second_low)
    site = dot3((first_high[...], first_low[...]), (swapped_high_ref[...], swapped_low_ref[...]), NT)

    @pl.when(step == 0)
    def _():
        site_ref[...] = site
        for copy in copies:
            copy.wait()

    @pl.when(step > 0)
    def _():
        site_ref[...] += site

    terms = dot3((second_high[...], second_low[...]), (cotangent_high[...], cotangent_low[...]), NT)
    place(terms, sources_ref, staged, ahead_ref, behind_ref, kept_ref)


def right_kernel(places_ref, back_high_ref, back_low_ref, edge_ref, own_ref, other_ref, turned_high, turned_low, placed):
    @pl.when(pl.program_id(0) == 0)
    def _():
        for chunk in range(CHUNKS):
            rows = slice(chunk * ROWS, (chunk + 1) * ROWS)
            turned_high[:, rows] = back_high_ref[rows, :].T
            turned_low[:, rows] = back_low_ref[rows, :].T

    terms = dot3((turned_high[...], turned_low[...]), split(edge_ref[...]), NN)
    for block in range(16):
        start = pl.multiple_of(places_ref[block], 64)
        placed[pl.ds(start, 64), :] = terms[64 * block : 64 * block + 64, :]
    own_ref[...] = placed[:512, :]
    other_ref[...] = placed[512:, :]


def resident(shape):
    return pl.BlockSpec(shape, lambda *_: (0,) * len(shape))


ANY = pl.BlockSpec(memory_space=pl.ANY)
SQUARE = jax.ShapeDtypeStruct((1024, 1024), BF16)
CHUNK = pl.BlockSpec((ROWS, 1024), lambda i, *_: (i, 0))


def back_call(offsets, pieces, rows, site_matrix):
    return pl.pallas_call(
        functools.partial(back_kernel, len(pieces)),
        out_shape=(SQUARE,) * 6,
        grid_spec=pltpu.PrefetchScalarGridSpec(
            num_scalar_prefetch=1,
            grid=(CHUNKS,),
            in_specs=[ANY] * len(pieces) + [CHUNK, resident((256, 256))],
            out_specs=[resident((1024, 1024))] * 2 + [CHUNK] * 4,
            scratch_shapes=[pltpu.VMEM((1024, 1024), F32), pltpu.SemaphoreType.DMA((16,))],
        ),
        compiler_params=PARAMS,
        name="back",
    )(offsets, *pieces, rows, site_matrix)


BLOCKS = tuple(jax.ShapeDtypeStruct((count, 2, 64, 1024), F32) for count in (2, 2, 4))
BLOCK_SPECS = [pl.BlockSpec((count, 2, 16, 1024), lambda i, *_: (0, 0, i, 0)) for count in (2, 2, 4)]


def edge_call(offsets, sources, pieces, back_split):
    return pl.pallas_call(
        functools.partial(edge_kernel, len(pieces)),
        out_shape=(SQUARE, SQUARE, *BLOCKS),
        grid_spec=pltpu.PrefetchScalarGridSpec(
            num_scalar_prefetch=2,
            grid=(CHUNKS,),
            in_specs=[ANY] * len(pieces) + [CHUNK, CHUNK],
            out_specs=[resident((1024, 1024))] * 2 + BLOCK_SPECS,
            scratch_shapes=[
                pltpu.VMEM((1024, 1024), F32),
                pltpu.VMEM((16, 16, 1024), F32),
                pltpu.SemaphoreType.DMA((16,)),
            ],
        ),
        compiler_params=PARAMS,
        name="edge",
    )(offsets, sources, *pieces, *back_split)


def left_call(sources, edge_rows, right_split, site_matrix, swapped_split, cotangent_split):
    return pl.pallas_call(
        left_kernel,
        out_shape=(*BLOCKS, jax.ShapeDtypeStruct((256, 256), F32)),
        grid_spec=pltpu.PrefetchScalarGridSpec(
            num_scalar_prefetch=1,
            grid=(CHUNKS,),
            in_specs=[CHUNK]
            + [resident((1024, 1024))] * 2
            + [resident((256, 256))]
            + [CHUNK] * 2
            + [ANY] * 2,
            out_specs=BLOCK_SPECS + [resident((256, 256))],
            scratch_shapes=[pltpu.VMEM((ROWS, 1024), BF16)] * 4
            + [pltpu.VMEM((1024, 1024), BF16)] * 2
            + [pltpu.VMEM((16, 16, 1024), F32), pltpu.SemaphoreType.DMA((2,))],
        ),
        compiler_params=PARAMS,
        name="left",
    )(sources, edge_rows, *right_split, site_matrix, *swapped_split, *cotangent_split)


def right_call(places, back_split, edge_rows):
    column = lambda rows: pl.BlockSpec((rows, 256), lambda i, *_: (0, i))
    return pl.pallas_call(
        right_kernel,
        out_shape=(jax.ShapeDtypeStruct((512, 1024), F32),) * 2,
        grid_spec=pltpu.PrefetchScalarGridSpec(
            num_scalar_prefetch=1,
            grid=(4,),
            in_specs=[resident((1024, 1024))] * 2 + [column(1024)],
            out_specs=[column(512)] * 2,
            scratch_shapes=[pltpu.VMEM((1024, 1024), BF16)] * 2 + [pltpu.VMEM((1024, 256), F32)],
        ),
        compiler_params=PARAMS,
        name="right",
    )(places, *back_split, edge_rows)


def row_permute(value, z, y, core):
    pairs = []
    for source in range(16):
        there = ((source // 8) ^ z) * 8 + ((source // 2 + y) % 4) * 2 + ((source % 2) ^ core)
        pairs.append((source, there))
    return lax.ppermute(value, "row", pairs)


def col_permute(value, z, x):
    return lax.ppermute(value, "col", [(i, ((i // 4) ^ z) * 4 + (i + x) % 4) for i in range(8)])


def col_reduce(ahead, behind, kept):
    from_behind = col_permute(ahead, 0, 1)
    from_ahead = col_permute(behind, 0, 3)
    far_behind = col_permute(kept[0] + from_behind[0], 0, 1)
    far_ahead = col_permute(kept[1] + from_ahead[0], 0, 3)
    other = kept[3] + from_behind[1] + far_ahead
    same = kept[2] + from_ahead[1] + far_behind
    return jnp.transpose(same + col_permute(other, 1, 0), (1, 0, 2))


def dense(value):
    cols, bond, width = value.shape
    return jnp.transpose(value.reshape(cols, 2, 8, width), (3, 2, 1, 0)).reshape(width, bond * cols)


def take(value, index):
    return lax.dynamic_index_in_dim(value, index, 0, keepdims=False)


def on_device(edge_tensor, site_tensor, left_isometry, right_isometry, cotangent):
    row = lax.axis_index("row").astype(jnp.int32)
    col = lax.axis_index("col").astype(jnp.int32)
    z, y, core = row >> 3, (row >> 1) & 3, row & 1
    edge_rows = edge_tensor.reshape(1024, 1024)
    left_rows = left_isometry.reshape(1024, 1024)

    def offset_of(other_z, steps, other_core):
        other_z, steps, other_core = (np.array(list(v), np.int32) for v in (other_z, steps, other_core))
        return ((z ^ other_z) * 8 + ((y - steps) & 3) * 2 + (core ^ other_core)) * 64

    early = dense(cotangent)
    early, right_isometry = lax.optimization_barrier((early, right_isometry))
    other = row_permute(early, 1, 0, 0)
    own = dense(right_isometry)
    others = [row_permute(own, 0, steps, 0) for steps in (1, 3, 2)]
    quad = jnp.concatenate([own, *others], 0)
    pair = jnp.concatenate([early, other], 0)

    site_matrix = jnp.transpose(site_tensor, (2, 1, 3, 0)).reshape(256, 256)
    near = [row_permute(pair, 0, steps, 0) for steps in (1, 3)]
    far = row_permute(pair, 0, 2, 0)
    quads = [quad, row_permute(quad, 1, 0, 0)]
    near[0], near[1], site_matrix = lax.optimization_barrier((*near, site_matrix))
    pieces = [pair, *near, far]
    pieces += [row_permute(piece, 0, 0, 1) for piece in pieces]
    order = [(j, steps, c) for c in (0, 1) for steps in (0, 1, 3, 2) for j in (0, 1)]
    cotangent_high, cotangent_low, *rest = back_call(offset_of(*zip(*order)), pieces, left_rows, site_matrix)
    back_split, swapped_split = rest[:2], rest[2:]

    quads += [row_permute(piece, 0, 0, 1) for piece in quads]
    order = [(j, steps, c) for c in (0, 1) for j in (0, 1) for steps in (0, 1, 3, 2)]
    steps = np.array([2, 1, 2, 3, 1, 3, 0, 0], np.int32)
    others = np.array([0, 1, 1, 0, 0, 1, 0, 1], np.int32)
    sources = ((col >> 2) ^ others) * 4 + ((col + steps) & 3)
    right_high, right_low, *edge_terms = edge_call(offset_of(*zip(*order)), sources, quads, back_split)
    edge_gradient = col_reduce(*edge_terms)
    *left_terms, site_terms = left_call(
        sources, edge_rows, (right_high, right_low), site_matrix, swapped_split, (cotangent_high, cotangent_low)
    )
    left_gradient = col_reduce(*left_terms)

    blocks = np.array([(i % 2) * 8 + i // 2 for i in range(16)], np.int32)
    places = ((blocks & 1) ^ core) * 8 + (((blocks >> 1) - y) & 3) * 2 + ((blocks >> 3) ^ z)
    right_own, right_other = right_call(places * 64, back_split, edge_rows)

    part = site_terms.reshape(2, 128, 256)
    other = row_permute(take(part, 1 - core), 0, 0, 1)
    part = (take(part, core) + other).reshape(2, 64, 256)
    other = row_permute(take(part, 1 - z), 1, 0, 0)
    part = (take(part, z) + other).reshape(4, 16, 256)
    part = take(part, y) + sum(row_permute(take(part, (y + k) & 3), 0, k, 0) for k in (1, 2, 3))
    part = part + sum(col_permute(part, 0, k) for k in (1, 2, 3))
    part = part + col_permute(part, 1, 0)
    ring = [part] + [row_permute(part, 0, k, 0) for k in (3, 2, 1)]
    part = lax.dynamic_slice_in_dim(jnp.concatenate(ring + ring, 0), ((4 - y) & 3) * 16, 64, 0)
    other = row_permute(part, 1, 0, 0)
    part = jnp.where(z == 0, jnp.concatenate([part, other], 0), jnp.concatenate([other, part], 0))
    other = row_permute(part, 0, 0, 1)
    part = jnp.where(core == 0, jnp.concatenate([part, other], 0), jnp.concatenate([other, part], 0))
    site_gradient = jnp.transpose(part.reshape(16, 16, 16, 16), (3, 1, 0, 2))

    total = (right_own + row_permute(right_other, 0, 0, 1)).reshape(4, 2, 64, 1024)
    total = total[0] + sum(row_permute(total[k], 0, k, 0) for k in (1, 3, 2))
    right_gradient = total[0] + row_permute(total[1], 1, 0, 0)

    return (
        edge_gradient,
        site_gradient,
        left_gradient,
        right_gradient.reshape(64, 1, 1024),
    )


def solution(mesh):
    in_specs = (
        P("row", None, None),
        P(),
        P("row", None, None),
        P("col", None, "row"),
        P("col", None, "row"),
    )
    out_specs = (P("row", "col", None), P(), P("row", "col", None), P("col", "row", None))

    return jax.shard_map(on_device, mesh=mesh, in_specs=in_specs, out_specs=out_specs, check_vma=False)
```

```python
import functools

import jax
import jax.numpy as jnp
import numpy as np
from jax import lax
from jax.experimental import pallas as pl
from jax.experimental.pallas import tpu as pltpu
from jax.sharding import PartitionSpec as P

F32, BF16 = jnp.float32, jnp.bfloat16
NN = (((1,), (0,)), ((), ()))
NT = (((1,), (1,)), ((), ()))
TN = (((0,), (0,)), ((), ()))
PARAMS = pltpu.CompilerParams(vmem_limit_bytes=60 << 20)
ROWS = 256
CHUNKS = 4


def split(value):
    high = value.astype(BF16)
    return high, (value - high.astype(F32)).astype(BF16)


def dot3(left, right, dims):
    dot = functools.partial(lax.dot_general, dimension_numbers=dims, preferred_element_type=F32)
    return dot(left[0], right[0]) + (dot(left[0], right[1]) + dot(left[1], right[0]))


def swap_into(value, high_ref, low_ref):
    lane = lax.broadcasted_iota(jnp.int32, (16, 128), 1)
    for pair in range(8):
        for tile in range(8):
            first = value[32 * pair : 32 * pair + 16, 128 * tile : 128 * tile + 128]
            second = value[32 * pair + 16 : 32 * pair + 32, 128 * tile : 128 * tile + 128]
            even = jnp.where(lane < 64, first, pltpu.roll(second, 64, 1))
            odd = jnp.where(lane < 64, pltpu.roll(first, 64, 1), second)
            columns = slice(128 * pair, 128 * pair + 128)
            for start, part in ((16 * tile, even), (128 + 16 * tile, odd)):
                high, low = split(part)
                high_ref[start : start + 16, columns] = high
                low_ref[start : start + 16, columns] = low


def unswap_into(value, high_ref, low_ref):
    lane = lax.broadcasted_iota(jnp.int32, (16, 128), 1)
    for pair in range(8):
        for tile in range(8):
            columns = slice(128 * pair, 128 * pair + 128)
            even = value[16 * tile : 16 * tile + 16, columns]
            odd = value[128 + 16 * tile : 128 + 16 * tile + 16, columns]
            first = jnp.where(lane < 64, even, pltpu.roll(odd, 64, 1))
            second = jnp.where(lane < 64, pltpu.roll(even, 64, 1), odd)
            columns = slice(128 * tile, 128 * tile + 128)
            for start, part in ((32 * pair, first), (32 * pair + 16, second)):
                high, low = split(part)
                high_ref[start : start + 16, columns] = high
                low_ref[start : start + 16, columns] = low


def assemble(offsets_ref, piece_refs, whole_ref, sems, high_ref, low_ref):
    block = 64
    copies = []
    count = 0
    for piece in piece_refs:
        for part in range(piece.shape[0] // block):
            start = pl.multiple_of(offsets_ref[count], block)
            target = whole_ref.at[pl.ds(start, block)]
            copies.append((pltpu.make_async_copy(piece.at[pl.ds(part * block, block)], target, sems.at[count]), start))
            count += 1
    for copy, _ in copies:
        copy.start()
    for copy, start in copies:
        copy.wait()

        def some(index, carry, start=start):
            rows = pl.ds(pl.multiple_of(start + index * 16, 16), 16)
            high, low = split(whole_ref[rows, :])
            high_ref[rows, :] = high
            low_ref[rows, :] = low
            return carry

        lax.fori_loop(0, block // 16, some, 0)


def back_kernel(pieces, offsets_ref, *refs):
    piece_refs = refs[:pieces]
    rows_ref, site_ref = refs[pieces : pieces + 2]
    whole_high, whole_low, back_high, back_low, swapped_high, swapped_low, whole, sems = refs[pieces + 2 :]

    @pl.when(pl.program_id(0) == 0)
    def _():
        assemble(offsets_ref, piece_refs, whole, sems, whole_high, whole_low)

    section = dot3(split(rows_ref[...]), (whole_high[...], whole_low[...]), NN)
    swap_into(section, swapped_high, swapped_low)
    mixed = dot3(split(site_ref[...]), (swapped_high[...], swapped_low[...]), NN)
    unswap_into(mixed, back_high, back_low)


def place(terms, sources_ref, staged, ahead_ref, behind_ref, kept_ref):
    for a in range(16):
        staged[:, a, :] = terms[16 * a : 16 * a + 16, :]
    slot = 0
    for ref in (ahead_ref, behind_ref, kept_ref):
        for block in range(ref.shape[0]):
            ref[block] = staged[pl.ds(sources_ref[slot] * 2, 2)]
            slot += 1


def edge_kernel(pieces, offsets_ref, sources_ref, *refs):
    piece_refs = refs[:pieces]
    back_high_ref, back_low_ref = refs[pieces : pieces + 2]
    whole_high, whole_low, ahead_ref, behind_ref, kept_ref, whole, staged, sems = refs[pieces + 2 :]

    @pl.when(pl.program_id(0) == 0)
    def _():
        assemble(offsets_ref, piece_refs, whole, sems, whole_high, whole_low)

    terms = dot3((back_high_ref[...], back_low_ref[...]), (whole_high[...], whole_low[...]), NT)
    place(terms, sources_ref, staged, ahead_ref, behind_ref, kept_ref)


def first_kernel(
    edge_ref,
    right_high_ref,
    right_low_ref,
    site_matrix_ref,
    swapped_high_ref,
    swapped_low_ref,
    second_high_ref,
    second_low_ref,
    site_ref,
    first_high,
    first_low,
):
    first = dot3(split(edge_ref[...]), (right_high_ref[...], right_low_ref[...]), NN)
    swap_into(first, first_high, first_low)
    mixed = dot3(split(site_matrix_ref[...]), (first_high[...], first_low[...]), TN)
    unswap_into(mixed, second_high_ref, second_low_ref)
    site = dot3((first_high[...], first_low[...]), (swapped_high_ref[...], swapped_low_ref[...]), NT)

    @pl.when(pl.program_id(0) == 0)
    def _():
        site_ref[...] = site

    @pl.when(pl.program_id(0) > 0)
    def _():
        site_ref[...] += site


def left_kernel(
    sources_ref, second_high_ref, second_low_ref, high_ref, low_ref, ahead_ref, behind_ref, kept_ref, staged
):
    terms = dot3((second_high_ref[...], second_low_ref[...]), (high_ref[...], low_ref[...]), NT)
    place(terms, sources_ref, staged, ahead_ref, behind_ref, kept_ref)


def right_kernel(places_ref, back_high_ref, back_low_ref, edge_ref, own_ref, other_ref, turned_high, turned_low, placed):
    @pl.when(pl.program_id(0) == 0)
    def _():
        for chunk in range(CHUNKS):
            rows = slice(chunk * ROWS, (chunk + 1) * ROWS)
            turned_high[:, rows] = back_high_ref[rows, :].T
            turned_low[:, rows] = back_low_ref[rows, :].T

    terms = dot3((turned_high[...], turned_low[...]), split(edge_ref[...]), NN)
    for block in range(16):
        start = pl.multiple_of(places_ref[block], 64)
        placed[pl.ds(start, 64), :] = terms[64 * block : 64 * block + 64, :]
    own_ref[...] = placed[:512, :]
    other_ref[...] = placed[512:, :]


def resident(shape):
    return pl.BlockSpec(shape, lambda *_: (0,) * len(shape))


ANY = pl.BlockSpec(memory_space=pl.ANY)
SQUARE = jax.ShapeDtypeStruct((1024, 1024), BF16)
CHUNK = pl.BlockSpec((ROWS, 1024), lambda i, *_: (i, 0))


def back_call(offsets, pieces, rows, site_matrix):
    return pl.pallas_call(
        functools.partial(back_kernel, len(pieces)),
        out_shape=(SQUARE,) * 6,
        grid_spec=pltpu.PrefetchScalarGridSpec(
            num_scalar_prefetch=1,
            grid=(CHUNKS,),
            in_specs=[ANY] * len(pieces) + [CHUNK, resident((256, 256))],
            out_specs=[resident((1024, 1024))] * 2 + [CHUNK] * 4,
            scratch_shapes=[pltpu.VMEM((1024, 1024), F32), pltpu.SemaphoreType.DMA((16,))],
        ),
        compiler_params=PARAMS,
        name="back",
    )(offsets, *pieces, rows, site_matrix)


BLOCKS = tuple(jax.ShapeDtypeStruct((count, 2, 64, 1024), F32) for count in (2, 2, 4))
BLOCK_SPECS = [pl.BlockSpec((count, 2, 16, 1024), lambda i, *_: (0, 0, i, 0)) for count in (2, 2, 4)]


def edge_call(offsets, sources, pieces, back_split):
    return pl.pallas_call(
        functools.partial(edge_kernel, len(pieces)),
        out_shape=(SQUARE, SQUARE, *BLOCKS),
        grid_spec=pltpu.PrefetchScalarGridSpec(
            num_scalar_prefetch=2,
            grid=(CHUNKS,),
            in_specs=[ANY] * len(pieces) + [CHUNK, CHUNK],
            out_specs=[resident((1024, 1024))] * 2 + BLOCK_SPECS,
            scratch_shapes=[
                pltpu.VMEM((1024, 1024), F32),
                pltpu.VMEM((16, 16, 1024), F32),
                pltpu.SemaphoreType.DMA((16,)),
            ],
        ),
        compiler_params=PARAMS,
        name="edge",
    )(offsets, sources, *pieces, *back_split)


def first_call(edge_rows, right_split, site_matrix, swapped_split):
    return pl.pallas_call(
        first_kernel,
        out_shape=(SQUARE, SQUARE, jax.ShapeDtypeStruct((256, 256), F32)),
        grid=(CHUNKS,),
        in_specs=[CHUNK] + [resident((1024, 1024))] * 2 + [resident((256, 256))] + [CHUNK] * 2,
        out_specs=[CHUNK, CHUNK, resident((256, 256))],
        scratch_shapes=[pltpu.VMEM((ROWS, 1024), BF16)] * 2,
        compiler_params=PARAMS,
        name="first",
    )(edge_rows, *right_split, site_matrix, *swapped_split)


def left_call(sources, second_split, cotangent_split):
    return pl.pallas_call(
        left_kernel,
        out_shape=BLOCKS,
        grid_spec=pltpu.PrefetchScalarGridSpec(
            num_scalar_prefetch=1,
            grid=(CHUNKS,),
            in_specs=[CHUNK] * 2 + [resident((1024, 1024))] * 2,
            out_specs=BLOCK_SPECS,
            scratch_shapes=[pltpu.VMEM((16, 16, 1024), F32)],
        ),
        compiler_params=PARAMS,
        name="left",
    )(sources, *second_split, *cotangent_split)


def right_call(places, back_split, edge_rows):
    column = lambda rows: pl.BlockSpec((rows, 256), lambda i, *_: (0, i))
    return pl.pallas_call(
        right_kernel,
        out_shape=(jax.ShapeDtypeStruct((512, 1024), F32),) * 2,
        grid_spec=pltpu.PrefetchScalarGridSpec(
            num_scalar_prefetch=1,
            grid=(4,),
            in_specs=[resident((1024, 1024))] * 2 + [column(1024)],
            out_specs=[column(512)] * 2,
            scratch_shapes=[pltpu.VMEM((1024, 1024), BF16)] * 2 + [pltpu.VMEM((1024, 256), F32)],
        ),
        compiler_params=PARAMS,
        name="right",
    )(places, *back_split, edge_rows)


def row_permute(value, z, y, core):
    pairs = []
    for source in range(16):
        there = ((source // 8) ^ z) * 8 + ((source // 2 + y) % 4) * 2 + ((source % 2) ^ core)
        pairs.append((source, there))
    return lax.ppermute(value, "row", pairs)


def col_permute(value, z, x):
    return lax.ppermute(value, "col", [(i, ((i // 4) ^ z) * 4 + (i + x) % 4) for i in range(8)])


def col_reduce(ahead, behind, kept):
    from_behind = col_permute(ahead, 0, 1)
    from_ahead = col_permute(behind, 0, 3)
    far_behind = col_permute(kept[0] + from_behind[0], 0, 1)
    far_ahead = col_permute(kept[1] + from_ahead[0], 0, 3)
    other = kept[3] + from_behind[1] + far_ahead
    same = kept[2] + from_ahead[1] + far_behind
    return jnp.transpose(same + col_permute(other, 1, 0), (1, 0, 2))


def dense(value):
    cols, bond, width = value.shape
    return jnp.transpose(value.reshape(cols, 2, 8, width), (3, 2, 1, 0)).reshape(width, bond * cols)


def take(value, index):
    return lax.dynamic_index_in_dim(value, index, 0, keepdims=False)


def on_device(edge_tensor, site_tensor, left_isometry, right_isometry, cotangent):
    row = lax.axis_index("row").astype(jnp.int32)
    col = lax.axis_index("col").astype(jnp.int32)
    z, y, core = row >> 3, (row >> 1) & 3, row & 1
    edge_rows = edge_tensor.reshape(1024, 1024)
    left_rows = left_isometry.reshape(1024, 1024)

    def offset_of(other_z, steps, other_core):
        other_z, steps, other_core = (np.array(list(v), np.int32) for v in (other_z, steps, other_core))
        return ((z ^ other_z) * 8 + ((y - steps) & 3) * 2 + (core ^ other_core)) * 64

    early = dense(cotangent)
    early, right_isometry = lax.optimization_barrier((early, right_isometry))
    other = row_permute(early, 1, 0, 0)
    nearest = [row_permute(early, 0, steps, 0) for steps in (1, 3, 2)]
    own = dense(right_isometry)
    pair = jnp.concatenate([own, row_permute(own, 1, 0, 0)], 0)
    pieces = [early, *nearest, other, *(row_permute(other, 0, steps, 0) for steps in (1, 3, 2))]
    pairs = [pair] + [row_permute(pair, 0, steps, 0) for steps in (1, 3, 2)]

    site_matrix = jnp.transpose(site_tensor, (2, 1, 3, 0)).reshape(256, 256)
    pieces[3], site_matrix = lax.optimization_barrier((pieces[3], site_matrix))
    pieces += [row_permute(piece, 0, 0, 1) for piece in pieces]
    order = [(j, steps, c) for c in (0, 1) for j in (0, 1) for steps in (0, 1, 3, 2)]
    cotangent_high, cotangent_low, *rest = back_call(offset_of(*zip(*order)), pieces, left_rows, site_matrix)
    back_split, swapped_split = rest[:2], rest[2:]

    pairs += [row_permute(piece, 0, 0, 1) for piece in pairs]
    order = [(j, steps, c) for c in (0, 1) for steps in (0, 1, 3, 2) for j in (0, 1)]
    steps = np.array([2, 1, 2, 3, 1, 3, 0, 0], np.int32)
    others = np.array([0, 1, 1, 0, 0, 1, 0, 1], np.int32)
    sources = ((col >> 2) ^ others) * 4 + ((col + steps) & 3)
    right_high, right_low, *edge_terms = edge_call(offset_of(*zip(*order)), sources, pairs, back_split)
    edge_gradient = col_reduce(*edge_terms)
    *second_split, site_terms = first_call(edge_rows, (right_high, right_low), site_matrix, swapped_split)
    left_terms = left_call(sources, second_split, (cotangent_high, cotangent_low))
    left_gradient = col_reduce(*left_terms)

    blocks = np.array([(i % 2) * 8 + i // 2 for i in range(16)], np.int32)
    places = ((blocks & 1) ^ core) * 8 + (((blocks >> 1) - y) & 3) * 2 + ((blocks >> 3) ^ z)
    right_own, right_other = right_call(places * 64, back_split, edge_rows)

    part = site_terms.reshape(2, 128, 256)
    other = row_permute(take(part, 1 - core), 0, 0, 1)
    part = (take(part, core) + other).reshape(2, 64, 256)
    other = row_permute(take(part, 1 - z), 1, 0, 0)
    part = (take(part, z) + other).reshape(4, 16, 256)
    part = take(part, y) + sum(row_permute(take(part, (y + k) & 3), 0, k, 0) for k in (1, 2, 3))
    part = part + sum(col_permute(part, 0, k) for k in (1, 2, 3))
    part = part + col_permute(part, 1, 0)
    ring = [part] + [row_permute(part, 0, k, 0) for k in (3, 2, 1)]
    part = lax.dynamic_slice_in_dim(jnp.concatenate(ring + ring, 0), ((4 - y) & 3) * 16, 64, 0)
    other = row_permute(part, 1, 0, 0)
    part = jnp.where(z == 0, jnp.concatenate([part, other], 0), jnp.concatenate([other, part], 0))
    other = row_permute(part, 0, 0, 1)
    part = jnp.where(core == 0, jnp.concatenate([part, other], 0), jnp.concatenate([other, part], 0))
    site_gradient = jnp.transpose(part.reshape(16, 16, 16, 16), (3, 1, 0, 2))

    total = (right_own + row_permute(right_other, 0, 0, 1)).reshape(4, 2, 64, 1024)
    total = total[0] + sum(row_permute(total[k], 0, k, 0) for k in (1, 3, 2))
    right_gradient = total[0] + row_permute(total[1], 1, 0, 0)

    return (
        edge_gradient,
        site_gradient,
        left_gradient,
        right_gradient.reshape(64, 1, 1024),
    )


def solution(mesh):
    in_specs = (
        P("row", None, None),
        P(),
        P("row", None, None),
        P("col", None, "row"),
        P("col", None, "row"),
    )
    out_specs = (P("row", "col", None), P(), P("row", "col", None), P("col", "row", None))

    return jax.shard_map(on_device, mesh=mesh, in_specs=in_specs, out_specs=out_specs, check_vma=False)
```

```python
import functools

import jax
import jax.numpy as jnp
import numpy as np
from jax import lax
from jax.experimental import pallas as pl
from jax.experimental.pallas import tpu as pltpu
from jax.sharding import PartitionSpec as P

F32, BF16 = jnp.float32, jnp.bfloat16
NN = (((1,), (0,)), ((), ()))
NT = (((1,), (1,)), ((), ()))
TN = (((0,), (0,)), ((), ()))
PARAMS = pltpu.CompilerParams(vmem_limit_bytes=28 << 20)
ROWS = 256
CHUNKS = 4


def split(value):
    high = value.astype(BF16)
    return high, (value - high.astype(F32)).astype(BF16)


def dot3(left, right, dims):
    dot = functools.partial(lax.dot_general, dimension_numbers=dims, preferred_element_type=F32)
    return dot(left[0], right[0]) + (dot(left[0], right[1]) + dot(left[1], right[0]))


def swap_into(value, high_ref, low_ref):
    lane = lax.broadcasted_iota(jnp.int32, (16, 128), 1)
    for pair in range(8):
        for tile in range(8):
            first = value[32 * pair : 32 * pair + 16, 128 * tile : 128 * tile + 128]
            second = value[32 * pair + 16 : 32 * pair + 32, 128 * tile : 128 * tile + 128]
            even = jnp.where(lane < 64, first, pltpu.roll(second, 64, 1))
            odd = jnp.where(lane < 64, pltpu.roll(first, 64, 1), second)
            columns = slice(128 * pair, 128 * pair + 128)
            for start, part in ((16 * tile, even), (128 + 16 * tile, odd)):
                high, low = split(part)
                high_ref[start : start + 16, columns] = high
                low_ref[start : start + 16, columns] = low


def unswap_into(value, high_ref, low_ref):
    lane = lax.broadcasted_iota(jnp.int32, (16, 128), 1)
    for pair in range(8):
        for tile in range(8):
            columns = slice(128 * pair, 128 * pair + 128)
            even = value[16 * tile : 16 * tile + 16, columns]
            odd = value[128 + 16 * tile : 128 + 16 * tile + 16, columns]
            first = jnp.where(lane < 64, even, pltpu.roll(odd, 64, 1))
            second = jnp.where(lane < 64, pltpu.roll(even, 64, 1), odd)
            columns = slice(128 * tile, 128 * tile + 128)
            for start, part in ((32 * pair, first), (32 * pair + 16, second)):
                high, low = split(part)
                high_ref[start : start + 16, columns] = high
                low_ref[start : start + 16, columns] = low


def assemble(offsets_ref, piece_refs, whole_ref, sems, high_ref, low_ref):
    block = 64
    copies = []
    count = 0
    for piece in piece_refs:
        for part in range(piece.shape[0] // block):
            start = pl.multiple_of(offsets_ref[count], block)
            target = whole_ref.at[pl.ds(start, block)]
            copies.append((pltpu.make_async_copy(piece.at[pl.ds(part * block, block)], target, sems.at[count]), start))
            count += 1
    for copy, _ in copies:
        copy.start()
    for copy, start in copies:
        copy.wait()

        def some(index, carry, start=start):
            rows = pl.ds(pl.multiple_of(start + index * 16, 16), 16)
            high, low = split(whole_ref[rows, :])
            high_ref[rows, :] = high
            low_ref[rows, :] = low
            return carry

        lax.fori_loop(0, block // 16, some, 0)


def chunk_of(ref):
    return ref.at[pl.ds(pl.multiple_of(pl.program_id(0) * ROWS, ROWS), ROWS)]


def back_kernel(pieces, offsets_ref, *refs):
    piece_refs = refs[:pieces]
    rows_ref, site_ref = refs[pieces : pieces + 2]
    whole_high, whole_low, back_high, back_low, swapped_high, swapped_low, whole, sems = refs[pieces + 2 :]

    @pl.when(pl.program_id(0) == 0)
    def _():
        assemble(offsets_ref, piece_refs, whole, sems, whole_high, whole_low)

    section = dot3(split(rows_ref[...]), (whole_high[...], whole_low[...]), NN)
    swapped_high, swapped_low = chunk_of(swapped_high), chunk_of(swapped_low)
    swap_into(section, swapped_high, swapped_low)
    mixed = dot3(split(site_ref[...]), (swapped_high[...], swapped_low[...]), NN)
    unswap_into(mixed, chunk_of(back_high), chunk_of(back_low))


def place(terms, sources_ref, staged, ahead_ref, behind_ref, kept_ref):
    for a in range(16):
        staged[:, a, :] = terms[16 * a : 16 * a + 16, :]
    slot = 0
    for ref in (ahead_ref, behind_ref, kept_ref):
        for block in range(ref.shape[0]):
            ref[block] = staged[pl.ds(sources_ref[slot] * 2, 2)]
            slot += 1


def edge_kernel(pieces, offsets_ref, sources_ref, *refs):
    piece_refs = refs[:pieces]
    back_high_ref, back_low_ref = refs[pieces : pieces + 2]
    whole_high, whole_low, ahead_ref, behind_ref, kept_ref, whole, staged, sems = refs[pieces + 2 :]

    @pl.when(pl.program_id(0) == 0)
    def _():
        assemble(offsets_ref, piece_refs, whole, sems, whole_high, whole_low)

    rows = chunk_of(back_high_ref)[...], chunk_of(back_low_ref)[...]
    terms = dot3(rows, (whole_high[...], whole_low[...]), NT)
    place(terms, sources_ref, staged, ahead_ref, behind_ref, kept_ref)


def first_kernel(
    edge_ref,
    right_high_ref,
    right_low_ref,
    site_matrix_ref,
    swapped_high_ref,
    swapped_low_ref,
    second_high_ref,
    second_low_ref,
    site_ref,
    first_high,
    first_low,
):
    first = dot3(split(edge_ref[...]), (right_high_ref[...], right_low_ref[...]), NN)
    swap_into(first, first_high, first_low)
    mixed = dot3(split(site_matrix_ref[...]), (first_high[...], first_low[...]), TN)
    unswap_into(mixed, chunk_of(second_high_ref), chunk_of(second_low_ref))
    swapped = chunk_of(swapped_high_ref)[...], chunk_of(swapped_low_ref)[...]
    site = dot3((first_high[...], first_low[...]), swapped, NT)

    @pl.when(pl.program_id(0) == 0)
    def _():
        site_ref[...] = site

    @pl.when(pl.program_id(0) > 0)
    def _():
        site_ref[...] += site


def left_kernel(
    sources_ref, second_high_ref, second_low_ref, high_ref, low_ref, ahead_ref, behind_ref, kept_ref, staged
):
    rows = chunk_of(second_high_ref)[...], chunk_of(second_low_ref)[...]
    terms = dot3(rows, (high_ref[...], low_ref[...]), NT)
    place(terms, sources_ref, staged, ahead_ref, behind_ref, kept_ref)


def right_kernel(places_ref, back_high_ref, back_low_ref, edge_ref, own_ref, other_ref, turned_high, turned_low, placed):
    @pl.when(pl.program_id(0) == 0)
    def _():
        for chunk in range(CHUNKS):
            rows = slice(chunk * ROWS, (chunk + 1) * ROWS)
            turned_high[:, rows] = back_high_ref[rows, :].T
            turned_low[:, rows] = back_low_ref[rows, :].T

    terms = dot3((turned_high[...], turned_low[...]), split(edge_ref[...]), NN)
    for block in range(16):
        start = pl.multiple_of(places_ref[block], 64)
        placed[pl.ds(start, 64), :] = terms[64 * block : 64 * block + 64, :]
    own_ref[...] = placed[:512, :]
    other_ref[...] = placed[512:, :]


def resident(shape):
    return pl.BlockSpec(shape, lambda *_: (0,) * len(shape))


ANY = pl.BlockSpec(memory_space=pl.ANY)
HELD = pl.BlockSpec(memory_space=pltpu.VMEM)
SQUARE = jax.ShapeDtypeStruct((1024, 1024), BF16)
CHUNK = pl.BlockSpec((ROWS, 1024), lambda i, *_: (i, 0))


def back_call(offsets, pieces, rows, site_matrix):
    return pl.pallas_call(
        functools.partial(back_kernel, len(pieces)),
        out_shape=(SQUARE,) * 6,
        grid_spec=pltpu.PrefetchScalarGridSpec(
            num_scalar_prefetch=1,
            grid=(CHUNKS,),
            in_specs=[ANY] * len(pieces) + [CHUNK, resident((256, 256))],
            out_specs=[HELD] * 6,
            scratch_shapes=[pltpu.VMEM((1024, 1024), F32), pltpu.SemaphoreType.DMA((16,))],
        ),
        compiler_params=PARAMS,
        name="back",
    )(offsets, *pieces, rows, site_matrix)


BLOCKS = tuple(jax.ShapeDtypeStruct((count, 2, 64, 1024), F32) for count in (2, 2, 4))
BLOCK_SPECS = [pl.BlockSpec((count, 2, 16, 1024), lambda i, *_: (0, 0, i, 0)) for count in (2, 2, 4)]


def edge_call(offsets, sources, pieces, back_split):
    return pl.pallas_call(
        functools.partial(edge_kernel, len(pieces)),
        out_shape=(SQUARE, SQUARE, *BLOCKS),
        grid_spec=pltpu.PrefetchScalarGridSpec(
            num_scalar_prefetch=2,
            grid=(CHUNKS,),
            in_specs=[ANY] * len(pieces) + [HELD, HELD],
            out_specs=[HELD] * 2 + BLOCK_SPECS,
            scratch_shapes=[
                pltpu.VMEM((1024, 1024), F32),
                pltpu.VMEM((16, 16, 1024), F32),
                pltpu.SemaphoreType.DMA((16,)),
            ],
        ),
        compiler_params=PARAMS,
        name="edge",
    )(offsets, sources, *pieces, *back_split)


def first_call(edge_rows, right_split, site_matrix, swapped_split):
    return pl.pallas_call(
        first_kernel,
        out_shape=(SQUARE, SQUARE, jax.ShapeDtypeStruct((256, 256), F32)),
        grid=(CHUNKS,),
        in_specs=[CHUNK] + [HELD] * 2 + [resident((256, 256))] + [HELD] * 2,
        out_specs=[HELD, HELD, resident((256, 256))],
        scratch_shapes=[pltpu.VMEM((ROWS, 1024), BF16)] * 2,
        compiler_params=PARAMS,
        name="first",
    )(edge_rows, *right_split, site_matrix, *swapped_split)


def left_call(sources, second_split, cotangent_split):
    return pl.pallas_call(
        left_kernel,
        out_shape=BLOCKS,
        grid_spec=pltpu.PrefetchScalarGridSpec(
            num_scalar_prefetch=1,
            grid=(CHUNKS,),
            in_specs=[HELD] * 4,
            out_specs=BLOCK_SPECS,
            scratch_shapes=[pltpu.VMEM((16, 16, 1024), F32)],
        ),
        compiler_params=PARAMS,
        name="left",
    )(sources, *second_split, *cotangent_split)


def right_call(places, back_split, edge_rows):
    column = lambda rows: pl.BlockSpec((rows, 256), lambda i, *_: (0, i))
    return pl.pallas_call(
        right_kernel,
        out_shape=(jax.ShapeDtypeStruct((512, 1024), F32),) * 2,
        grid_spec=pltpu.PrefetchScalarGridSpec(
            num_scalar_prefetch=1,
            grid=(4,),
            in_specs=[HELD] * 2 + [column(1024)],
            out_specs=[column(512)] * 2,
            scratch_shapes=[pltpu.VMEM((1024, 1024), BF16)] * 2 + [pltpu.VMEM((1024, 256), F32)],
        ),
        compiler_params=PARAMS,
        name="right",
    )(places, *back_split, edge_rows)


def row_permute(value, z, y, core):
    pairs = []
    for source in range(16):
        there = ((source // 8) ^ z) * 8 + ((source // 2 + y) % 4) * 2 + ((source % 2) ^ core)
        pairs.append((source, there))
    return lax.ppermute(value, "row", pairs)


def col_permute(value, z, x):
    return lax.ppermute(value, "col", [(i, ((i // 4) ^ z) * 4 + (i + x) % 4) for i in range(8)])


def col_reduce(ahead, behind, kept):
    from_behind = col_permute(ahead, 0, 1)
    from_ahead = col_permute(behind, 0, 3)
    far_behind = col_permute(kept[0] + from_behind[0], 0, 1)
    far_ahead = col_permute(kept[1] + from_ahead[0], 0, 3)
    other = kept[3] + from_behind[1] + far_ahead
    same = kept[2] + from_ahead[1] + far_behind
    return jnp.transpose(same + col_permute(other, 1, 0), (1, 0, 2))


def dense(value):
    cols, bond, width = value.shape
    return jnp.transpose(value.reshape(cols, 2, 8, width), (3, 2, 1, 0)).reshape(width, bond * cols)


def take(value, index):
    return lax.dynamic_index_in_dim(value, index, 0, keepdims=False)


def on_device(edge_tensor, site_tensor, left_isometry, right_isometry, cotangent):
    row = lax.axis_index("row").astype(jnp.int32)
    col = lax.axis_index("col").astype(jnp.int32)
    z, y, core = row >> 3, (row >> 1) & 3, row & 1
    edge_rows = edge_tensor.reshape(1024, 1024)
    left_rows = left_isometry.reshape(1024, 1024)

    def offset_of(other_z, steps, other_core):
        other_z, steps, other_core = (np.array(list(v), np.int32) for v in (other_z, steps, other_core))
        return ((z ^ other_z) * 8 + ((y - steps) & 3) * 2 + (core ^ other_core)) * 64

    early = dense(cotangent)
    early, right_isometry = lax.optimization_barrier((early, right_isometry))
    other = row_permute(early, 1, 0, 0)
    nearest = [row_permute(early, 0, steps, 0) for steps in (1, 3, 2)]
    own = dense(right_isometry)
    pair = jnp.concatenate([own, row_permute(own, 1, 0, 0)], 0)
    pieces = [early, *nearest, other, *(row_permute(other, 0, steps, 0) for steps in (1, 3, 2))]
    pairs = [pair] + [row_permute(pair, 0, steps, 0) for steps in (1, 3, 2)]

    site_matrix = jnp.transpose(site_tensor, (2, 1, 3, 0)).reshape(256, 256)
    pieces[3], site_matrix = lax.optimization_barrier((pieces[3], site_matrix))
    pieces += [row_permute(piece, 0, 0, 1) for piece in pieces]
    order = [(j, steps, c) for c in (0, 1) for j in (0, 1) for steps in (0, 1, 3, 2)]
    cotangent_high, cotangent_low, *rest = back_call(offset_of(*zip(*order)), pieces, left_rows, site_matrix)
    back_split, swapped_split = rest[:2], rest[2:]

    pairs += [row_permute(piece, 0, 0, 1) for piece in pairs]
    order = [(j, steps, c) for c in (0, 1) for steps in (0, 1, 3, 2) for j in (0, 1)]
    steps = np.array([2, 1, 2, 3, 1, 3, 0, 0], np.int32)
    others = np.array([0, 1, 1, 0, 0, 1, 0, 1], np.int32)
    sources = ((col >> 2) ^ others) * 4 + ((col + steps) & 3)
    right_high, right_low, *edge_terms = edge_call(offset_of(*zip(*order)), sources, pairs, back_split)
    edge_gradient = col_reduce(*edge_terms)
    *second_split, site_terms = first_call(edge_rows, (right_high, right_low), site_matrix, swapped_split)
    left_terms = left_call(sources, second_split, (cotangent_high, cotangent_low))
    left_gradient = col_reduce(*left_terms)

    blocks = np.array([(i % 2) * 8 + i // 2 for i in range(16)], np.int32)
    places = ((blocks & 1) ^ core) * 8 + (((blocks >> 1) - y) & 3) * 2 + ((blocks >> 3) ^ z)
    right_own, right_other = right_call(places * 64, back_split, edge_rows)

    me = core * 2 + z
    part = site_terms.reshape(4, 64, 256)
    part = take(part, me) + sum(row_permute(take(part, me ^ k), k & 1, 0, k >> 1) for k in (1, 2, 3))
    part = part.reshape(4, 16, 256)
    part = take(part, y) + sum(row_permute(take(part, (y + k) & 3), 0, k, 0) for k in (1, 2, 3))
    part = part + sum(col_permute(part, 0, k) for k in (1, 2, 3))
    part = part + col_permute(part, 1, 0)
    ring = [part] + [row_permute(part, 0, k, 0) for k in (3, 2, 1)]
    part = lax.dynamic_slice_in_dim(jnp.concatenate(ring + ring, 0), ((4 - y) & 3) * 16, 64, 0)
    near, across, far = (row_permute(part, k & 1, 0, k >> 1) for k in (1, 2, 3))
    low = jnp.where(z == 0, jnp.concatenate([part, near], 0), jnp.concatenate([near, part], 0))
    high = jnp.where(z == 0, jnp.concatenate([across, far], 0), jnp.concatenate([far, across], 0))
    part = jnp.where(core == 0, jnp.concatenate([low, high], 0), jnp.concatenate([high, low], 0))
    site_gradient = jnp.transpose(part.reshape(16, 16, 16, 16), (3, 1, 0, 2))

    right_own = right_own.reshape(4, 2, 64, 1024)
    received = row_permute(right_other, 0, 0, 1).reshape(4, 2, 64, 1024)
    total = [right_own[k] + received[k] for k in range(4)]
    total = total[0] + sum(row_permute(total[k], 0, k, 0) for k in (1, 3, 2))
    right_gradient = total[0] + row_permute(total[1], 1, 0, 0)

    return (
        edge_gradient,
        site_gradient,
        left_gradient,
        right_gradient.reshape(64, 1, 1024),
    )


def solution(mesh):
    in_specs = (
        P("row", None, None),
        P(),
        P("row", None, None),
        P("col", None, "row"),
        P("col", None, "row"),
    )
    out_specs = (P("row", "col", None), P(), P("row", "col", None), P("col", "row", None))

    return jax.shard_map(on_device, mesh=mesh, in_specs=in_specs, out_specs=out_specs, check_vma=False)
```

```python
import functools

import jax
import jax.numpy as jnp
import numpy as np
from jax import lax
from jax.experimental import pallas as pl
from jax.experimental.pallas import tpu as pltpu
from jax.sharding import PartitionSpec as P

F32, BF16 = jnp.float32, jnp.bfloat16
NN = (((1,), (0,)), ((), ()))
NT = (((1,), (1,)), ((), ()))
TN = (((0,), (0,)), ((), ()))
PARAMS = pltpu.CompilerParams(vmem_limit_bytes=28 << 20)
ROWS = 256
CHUNKS = 4
WIDTH = 512


def split(value):
    high = value.astype(BF16)
    return high, (value - high.astype(F32)).astype(BF16)


def dot3(left, right, dims):
    dot = functools.partial(lax.dot_general, dimension_numbers=dims, preferred_element_type=F32)
    return dot(left[0], right[0]) + (dot(left[0], right[1]) + dot(left[1], right[0]))


def swap_into(value, high_ref, low_ref):
    lane = lax.broadcasted_iota(jnp.int32, (16, 128), 1)
    for pair in range(8):
        for tile in range(8):
            first = value[32 * pair : 32 * pair + 16, 128 * tile : 128 * tile + 128]
            second = value[32 * pair + 16 : 32 * pair + 32, 128 * tile : 128 * tile + 128]
            even = jnp.where(lane < 64, first, pltpu.roll(second, 64, 1))
            odd = jnp.where(lane < 64, pltpu.roll(first, 64, 1), second)
            columns = slice(128 * pair, 128 * pair + 128)
            for start, part in ((16 * tile, even), (128 + 16 * tile, odd)):
                high, low = split(part)
                high_ref[start : start + 16, columns] = high
                low_ref[start : start + 16, columns] = low


def unswap_into(value, high_ref, low_ref):
    lane = lax.broadcasted_iota(jnp.int32, (16, 128), 1)
    for pair in range(8):
        for tile in range(8):
            columns = slice(128 * pair, 128 * pair + 128)
            even = value[16 * tile : 16 * tile + 16, columns]
            odd = value[128 + 16 * tile : 128 + 16 * tile + 16, columns]
            first = jnp.where(lane < 64, even, pltpu.roll(odd, 64, 1))
            second = jnp.where(lane < 64, pltpu.roll(even, 64, 1), odd)
            columns = slice(128 * tile, 128 * tile + 128)
            for start, part in ((32 * pair, first), (32 * pair + 16, second)):
                high, low = split(part)
                high_ref[start : start + 16, columns] = high
                low_ref[start : start + 16, columns] = low


def assemble(offsets_ref, piece_refs, whole_ref, sems, high_ref, low_ref):
    block = 64
    copies = []
    count = 0
    for piece in piece_refs:
        for part in range(piece.shape[0] // block):
            start = pl.multiple_of(offsets_ref[count], block)
            target = whole_ref.at[pl.ds(start, block)]
            copies.append((pltpu.make_async_copy(piece.at[pl.ds(part * block, block)], target, sems.at[count]), start))
            count += 1
    for copy, _ in copies:
        copy.start()
    for copy, start in copies:
        copy.wait()

        def some(index, carry, start=start):
            rows = pl.ds(pl.multiple_of(start + index * 16, 16), 16)
            high, low = split(whole_ref[rows, :])
            high_ref[rows, :] = high
            low_ref[rows, :] = low
            return carry

        lax.fori_loop(0, block // 16, some, 0)


def chunk_of(ref):
    return ref.at[pl.ds(pl.multiple_of(pl.program_id(0) * ROWS, ROWS), ROWS)]


def back_kernel(pieces, offsets_ref, *refs):
    piece_refs = refs[:pieces]
    rows_ref, site_ref = refs[pieces : pieces + 2]
    whole_high, whole_low, back_high, back_low, swapped_high, swapped_low, whole, sems = refs[pieces + 2 :]

    @pl.when(pl.program_id(0) == 0)
    def _():
        assemble(offsets_ref, piece_refs, whole, sems, whole_high, whole_low)

    section = dot3(split(rows_ref[...]), (whole_high[...], whole_low[...]), NN)
    swapped_high, swapped_low = chunk_of(swapped_high), chunk_of(swapped_low)
    swap_into(section, swapped_high, swapped_low)
    mixed = dot3(split(site_ref[...]), (swapped_high[...], swapped_low[...]), NN)
    unswap_into(mixed, chunk_of(back_high), chunk_of(back_low))


def block_of(ref):
    return ref.at[pl.ds(pl.multiple_of(pl.program_id(1) * WIDTH, WIDTH), WIDTH)]


def place(terms, sources_ref, staged, ahead_ref, behind_ref, kept_ref):
    for a in range(16):
        staged[:, a, :] = terms[16 * a : 16 * a + 16, :]
    slot = 0
    for ref in (ahead_ref, behind_ref, kept_ref):
        for block in range(ref.shape[0]):
            ref[block] = staged[pl.ds(sources_ref[slot] * 2, 2)]
            slot += 1


def edge_kernel(pieces, offsets_ref, sources_ref, *refs):
    piece_refs = refs[:pieces]
    back_high_ref, back_low_ref = refs[pieces : pieces + 2]
    whole_high, whole_low, ahead_ref, behind_ref, kept_ref, whole, staged, sems = refs[pieces + 2 :]

    @pl.when((pl.program_id(0) == 0) & (pl.program_id(1) == 0))
    def _():
        assemble(offsets_ref, piece_refs, whole, sems, whole_high, whole_low)

    rows = chunk_of(back_high_ref)[...], chunk_of(back_low_ref)[...]
    terms = dot3(rows, (block_of(whole_high)[...], block_of(whole_low)[...]), NT)
    place(terms, sources_ref, staged, ahead_ref, behind_ref, kept_ref)


def first_kernel(
    edge_ref,
    right_high_ref,
    right_low_ref,
    site_matrix_ref,
    swapped_high_ref,
    swapped_low_ref,
    second_high_ref,
    second_low_ref,
    site_ref,
    first_high,
    first_low,
):
    first = dot3(split(edge_ref[...]), (right_high_ref[...], right_low_ref[...]), NN)
    swap_into(first, first_high, first_low)
    mixed = dot3(split(site_matrix_ref[...]), (first_high[...], first_low[...]), TN)
    unswap_into(mixed, chunk_of(second_high_ref), chunk_of(second_low_ref))
    swapped = chunk_of(swapped_high_ref)[...], chunk_of(swapped_low_ref)[...]
    site = dot3((first_high[...], first_low[...]), swapped, NT)

    @pl.when(pl.program_id(0) == 0)
    def _():
        site_ref[...] = site

    @pl.when(pl.program_id(0) > 0)
    def _():
        site_ref[...] += site


def left_kernel(
    sources_ref, second_high_ref, second_low_ref, high_ref, low_ref, ahead_ref, behind_ref, kept_ref, staged
):
    rows = chunk_of(second_high_ref)[...], chunk_of(second_low_ref)[...]
    terms = dot3(rows, (block_of(high_ref)[...], block_of(low_ref)[...]), NT)
    place(terms, sources_ref, staged, ahead_ref, behind_ref, kept_ref)


def right_kernel(places_ref, back_high_ref, back_low_ref, edge_ref, own_ref, other_ref, turned_high, turned_low, placed):
    @pl.when(pl.program_id(0) == 0)
    def _():
        def turn(chunk, carry):
            rows = pl.ds(pl.multiple_of(chunk * ROWS, ROWS), ROWS)
            turned_high[:, rows] = back_high_ref[rows, :].T
            turned_low[:, rows] = back_low_ref[rows, :].T
            return carry

        lax.fori_loop(0, CHUNKS, turn, 0)

    terms = dot3((turned_high[...], turned_low[...]), split(edge_ref[...]), NN)
    for block in range(16):
        start = pl.multiple_of(places_ref[block], 64)
        placed[pl.ds(start, 64), :] = terms[64 * block : 64 * block + 64, :]
    own_ref[...] = placed[:512, :]
    other_ref[...] = placed[512:, :]


def resident(shape):
    return pl.BlockSpec(shape, lambda *_: (0,) * len(shape))


OUTSIDE = pl.BlockSpec(memory_space=pltpu.HBM)
HELD = pl.BlockSpec(memory_space=pltpu.VMEM)
SQUARE = jax.ShapeDtypeStruct((1024, 1024), BF16)
CHUNK = pl.BlockSpec((ROWS, 1024), lambda i, *_: (i, 0))


def back_call(offsets, pieces, rows, site_matrix):
    return pl.pallas_call(
        functools.partial(back_kernel, len(pieces)),
        out_shape=(SQUARE,) * 6,
        grid_spec=pltpu.PrefetchScalarGridSpec(
            num_scalar_prefetch=1,
            grid=(CHUNKS,),
            in_specs=[OUTSIDE] * len(pieces) + [CHUNK, resident((256, 256))],
            out_specs=[HELD] * 6,
            scratch_shapes=[pltpu.VMEM((1024, 1024), F32), pltpu.SemaphoreType.DMA((16,))],
        ),
        compiler_params=PARAMS,
        name="back",
    )(offsets, *pieces, rows, site_matrix)


BLOCKS = tuple(jax.ShapeDtypeStruct((count, 2, 64, 1024), F32) for count in (2, 2, 4))
BLOCK_SPECS = [pl.BlockSpec((count, 2, 16, WIDTH), lambda i, j, *_: (0, 0, i, j)) for count in (2, 2, 4)]


def edge_call(offsets, sources, pieces, back_split):
    return pl.pallas_call(
        functools.partial(edge_kernel, len(pieces)),
        out_shape=(SQUARE, SQUARE, *BLOCKS),
        grid_spec=pltpu.PrefetchScalarGridSpec(
            num_scalar_prefetch=2,
            grid=(CHUNKS, 1024 // WIDTH),
            in_specs=[OUTSIDE] * len(pieces) + [HELD, HELD],
            out_specs=[HELD] * 2 + BLOCK_SPECS,
            scratch_shapes=[
                pltpu.VMEM((1024, 1024), F32),
                pltpu.VMEM((16, 16, WIDTH), F32),
                pltpu.SemaphoreType.DMA((16,)),
            ],
        ),
        compiler_params=PARAMS,
        name="edge",
    )(offsets, sources, *pieces, *back_split)


def first_call(edge_rows, right_split, site_matrix, swapped_split):
    return pl.pallas_call(
        first_kernel,
        out_shape=(SQUARE, SQUARE, jax.ShapeDtypeStruct((256, 256), F32)),
        grid=(CHUNKS,),
        in_specs=[CHUNK] + [HELD] * 2 + [resident((256, 256))] + [HELD] * 2,
        out_specs=[HELD, HELD, resident((256, 256))],
        scratch_shapes=[pltpu.VMEM((ROWS, 1024), BF16)] * 2,
        compiler_params=PARAMS,
        name="first",
    )(edge_rows, *right_split, site_matrix, *swapped_split)


def left_call(sources, second_split, cotangent_split):
    return pl.pallas_call(
        left_kernel,
        out_shape=BLOCKS,
        grid_spec=pltpu.PrefetchScalarGridSpec(
            num_scalar_prefetch=1,
            grid=(CHUNKS, 1024 // WIDTH),
            in_specs=[HELD] * 4,
            out_specs=BLOCK_SPECS,
            scratch_shapes=[pltpu.VMEM((16, 16, WIDTH), F32)],
        ),
        compiler_params=PARAMS,
        name="left",
    )(sources, *second_split, *cotangent_split)


def right_call(places, back_split, edge_rows):
    column = lambda rows: pl.BlockSpec((rows, 256), lambda i, *_: (0, i))
    return pl.pallas_call(
        right_kernel,
        out_shape=(jax.ShapeDtypeStruct((512, 1024), F32),) * 2,
        grid_spec=pltpu.PrefetchScalarGridSpec(
            num_scalar_prefetch=1,
            grid=(4,),
            in_specs=[HELD] * 2 + [column(1024)],
            out_specs=[column(512)] * 2,
            scratch_shapes=[pltpu.VMEM((1024, 1024), BF16)] * 2 + [pltpu.VMEM((1024, 256), F32)],
        ),
        compiler_params=PARAMS,
        name="right",
    )(places, *back_split, edge_rows)


def row_permute(value, z, y, core):
    pairs = []
    for source in range(16):
        there = ((source // 8) ^ z) * 8 + ((source // 2 + y) % 4) * 2 + ((source % 2) ^ core)
        pairs.append((source, there))
    return lax.ppermute(value, "row", pairs)


def col_permute(value, z, x):
    return lax.ppermute(value, "col", [(i, ((i // 4) ^ z) * 4 + (i + x) % 4) for i in range(8)])


def col_reduce(ahead, behind, kept):
    from_behind = col_permute(ahead, 0, 1)
    from_ahead = col_permute(behind, 0, 3)
    far_behind = col_permute(kept[0] + from_behind[0], 0, 1)
    far_ahead = col_permute(kept[1] + from_ahead[0], 0, 3)
    other = kept[3] + from_behind[1] + far_ahead
    same = kept[2] + from_ahead[1] + far_behind
    return jnp.transpose(same + col_permute(other, 1, 0), (1, 0, 2))


def dense(value):
    cols, bond, width = value.shape
    return jnp.transpose(value.reshape(cols, 2, 8, width), (3, 2, 1, 0)).reshape(width, bond * cols)


def take(value, index):
    return lax.dynamic_index_in_dim(value, index, 0, keepdims=False, allow_negative_indices=False)


def on_device(edge_tensor, site_tensor, left_isometry, right_isometry, cotangent):
    row = lax.axis_index("row").astype(jnp.int32)
    col = lax.axis_index("col").astype(jnp.int32)
    z, y, core = row >> 3, (row >> 1) & 3, row & 1
    edge_rows = edge_tensor.reshape(1024, 1024)
    left_rows = left_isometry.reshape(1024, 1024)

    def offset_of(other_z, steps, other_core):
        other_z, steps, other_core = (np.array(list(v), np.int32) for v in (other_z, steps, other_core))
        return ((z ^ other_z) * 8 + ((y - steps) & 3) * 2 + (core ^ other_core)) * 64

    site_matrix = jnp.transpose(site_tensor, (2, 1, 3, 0)).reshape(256, 256)
    order = [(j, steps, c) for c in (0, 1) for j in (0, 1) for steps in (0, 1, 3, 2)]
    cotangent_offsets = offset_of(*zip(*order))
    order = [(j, steps, c) for c in (0, 1) for steps in (0, 1, 3, 2) for j in (0, 1)]
    isometry_offsets = offset_of(*zip(*order))
    steps = np.array([2, 1, 2, 3, 1, 3, 0, 0], np.int32)
    others = np.array([0, 1, 1, 0, 0, 1, 0, 1], np.int32)
    sources = ((col >> 2) ^ others) * 4 + ((col + steps) & 3)
    blocks = np.array([(i % 2) * 8 + i // 2 for i in range(16)], np.int32)
    places = (((blocks & 1) ^ core) * 8 + (((blocks >> 1) - y) & 3) * 2 + ((blocks >> 3) ^ z)) * 64
    corners = [(core * 2 + z) ^ k for k in range(4)]
    ahead = [(y + k) & 3 for k in range(4)]
    first_row, at_low_z, at_low_core = ((4 - y) & 3) * 16, z == 0, core == 0

    early = dense(cotangent)
    early, right_isometry = lax.optimization_barrier((early, right_isometry))
    other = row_permute(early, 1, 0, 0)
    nearest = [row_permute(early, 0, steps, 0) for steps in (1, 3, 2)]
    values = (site_matrix, cotangent_offsets, isometry_offsets, sources, places)
    indices = (*corners, *ahead, first_row, at_low_z, at_low_core)
    other, values, indices = lax.optimization_barrier((other, values, indices))
    site_matrix, cotangent_offsets, isometry_offsets, sources, places = values
    corners, ahead, (first_row, at_low_z, at_low_core) = indices[:4], indices[4:8], indices[8:]
    own = dense(right_isometry)
    pair = jnp.concatenate([own, row_permute(own, 1, 0, 0)], 0)
    pieces = [early, *nearest, other, *(row_permute(other, 0, steps, 0) for steps in (1, 3, 2))]
    pairs = [pair] + [row_permute(pair, 0, steps, 0) for steps in (1, 3, 2)]

    pieces += [row_permute(piece, 0, 0, 1) for piece in pieces]
    cotangent_high, cotangent_low, *rest = back_call(cotangent_offsets, pieces, left_rows, site_matrix)
    back_split, swapped_split = rest[:2], rest[2:]

    pairs += [row_permute(piece, 0, 0, 1) for piece in pairs]
    right_high, right_low, *edge_terms = edge_call(isometry_offsets, sources, pairs, back_split)
    edge_gradient = col_reduce(*edge_terms)
    *second_split, site_terms = first_call(edge_rows, (right_high, right_low), site_matrix, swapped_split)
    left_terms = left_call(sources, second_split, (cotangent_high, cotangent_low))
    left_gradient = col_reduce(*left_terms)

    right_own, right_other = right_call(places, back_split, edge_rows)

    part = site_terms.reshape(4, 64, 256)
    sends = [row_permute(take(part, corners[k]), k & 1, 0, k >> 1) for k in (1, 2, 3)]
    part = take(part, corners[0]) + sum(sends)
    part = part.reshape(4, 16, 256)
    part = take(part, ahead[0]) + sum(row_permute(take(part, ahead[k]), 0, k, 0) for k in (1, 2, 3))
    part = part + sum(col_permute(part, 0, k) for k in (1, 2, 3))
    part = part + col_permute(part, 1, 0)
    ring = [part] + [row_permute(part, 0, k, 0) for k in (3, 2, 1)]
    ring = jnp.concatenate(ring + ring, 0)
    part = lax.dynamic_slice(ring, (first_row, 0), (64, 256), allow_negative_indices=False)
    near, across, far = (row_permute(part, k & 1, 0, k >> 1) for k in (1, 2, 3))
    low = jnp.where(at_low_z, jnp.concatenate([part, near], 0), jnp.concatenate([near, part], 0))
    high = jnp.where(at_low_z, jnp.concatenate([across, far], 0), jnp.concatenate([far, across], 0))
    part = jnp.where(at_low_core, jnp.concatenate([low, high], 0), jnp.concatenate([high, low], 0))
    site_gradient = jnp.transpose(part.reshape(16, 16, 16, 16), (3, 1, 0, 2))

    right_own = right_own.reshape(4, 2, 64, 1024)
    received = row_permute(right_other, 0, 0, 1).reshape(4, 2, 64, 1024)
    total = [right_own[k] + received[k] for k in range(4)]
    total = total[0] + sum(row_permute(total[k], 0, k, 0) for k in (1, 3, 2))
    right_gradient = total[0] + row_permute(total[1], 1, 0, 0)

    return (
        edge_gradient,
        site_gradient,
        left_gradient,
        right_gradient.reshape(64, 1, 1024),
    )


def solution(mesh):
    in_specs = (
        P("row", None, None),
        P(),
        P("row", None, None),
        P("col", None, "row"),
        P("col", None, "row"),
    )
    out_specs = (P("row", "col", None), P(), P("row", "col", None), P("col", "row", None))

    return jax.shard_map(on_device, mesh=mesh, in_specs=in_specs, out_specs=out_specs, check_vma=False)
```

```python
import functools

import jax
import jax.numpy as jnp
import numpy as np
from jax import lax
from jax.experimental import pallas as pl
from jax.experimental.pallas import tpu as pltpu
from jax.sharding import PartitionSpec as P

F32, BF16 = jnp.float32, jnp.bfloat16
NN = (((1,), (0,)), ((), ()))
NT = (((1,), (1,)), ((), ()))
TN = (((0,), (0,)), ((), ()))
PARAMS = pltpu.CompilerParams(vmem_limit_bytes=28 << 20)
ROWS = 256
CHUNKS = 4
WIDTH = 512


def split(value):
    high = value.astype(BF16)
    return high, (value - high.astype(F32)).astype(BF16)


def dot3(left, right, dims):
    dot = functools.partial(lax.dot_general, dimension_numbers=dims, preferred_element_type=F32)
    return dot(left[0], right[0]) + (dot(left[0], right[1]) + dot(left[1], right[0]))


def swap_into(value, high_ref, low_ref):
    lane = lax.broadcasted_iota(jnp.int32, (16, 128), 1)
    for pair in range(8):
        for tile in range(8):
            first = value[32 * pair : 32 * pair + 16, 128 * tile : 128 * tile + 128]
            second = value[32 * pair + 16 : 32 * pair + 32, 128 * tile : 128 * tile + 128]
            even = jnp.where(lane < 64, first, pltpu.roll(second, 64, 1))
            odd = jnp.where(lane < 64, pltpu.roll(first, 64, 1), second)
            columns = slice(128 * pair, 128 * pair + 128)
            for start, part in ((16 * tile, even), (128 + 16 * tile, odd)):
                high, low = split(part)
                high_ref[start : start + 16, columns] = high
                low_ref[start : start + 16, columns] = low


def unswap_into(value, high_ref, low_ref):
    lane = lax.broadcasted_iota(jnp.int32, (16, 128), 1)
    for pair in range(8):
        for tile in range(8):
            columns = slice(128 * pair, 128 * pair + 128)
            even = value[16 * tile : 16 * tile + 16, columns]
            odd = value[128 + 16 * tile : 128 + 16 * tile + 16, columns]
            first = jnp.where(lane < 64, even, pltpu.roll(odd, 64, 1))
            second = jnp.where(lane < 64, pltpu.roll(even, 64, 1), odd)
            columns = slice(128 * tile, 128 * tile + 128)
            for start, part in ((32 * pair, first), (32 * pair + 16, second)):
                high, low = split(part)
                high_ref[start : start + 16, columns] = high
                low_ref[start : start + 16, columns] = low


def assemble(offsets_ref, piece_refs, whole_ref, sems, high_ref, low_ref):
    block = 64
    copies = []
    count = 0
    for piece in piece_refs:
        for part in range(piece.shape[0] // block):
            start = pl.multiple_of(offsets_ref[count], block)
            target = whole_ref.at[pl.ds(start, block)]
            copies.append((pltpu.make_async_copy(piece.at[pl.ds(part * block, block)], target, sems.at[count]), start))
            count += 1
    for copy, _ in copies:
        copy.start()
    for copy, start in copies:
        copy.wait()

        def some(index, carry, start=start):
            rows = pl.ds(pl.multiple_of(start + index * 16, 16), 16)
            high, low = split(whole_ref[rows, :])
            high_ref[rows, :] = high
            low_ref[rows, :] = low
            return carry

        lax.fori_loop(0, block // 16, some, 0)


def chunk_of(ref):
    return ref.at[pl.ds(pl.multiple_of(pl.program_id(0) * ROWS, ROWS), ROWS)]


def back_kernel(pieces, offsets_ref, *refs):
    piece_refs = refs[:pieces]
    rows_ref, site_ref = refs[pieces : pieces + 2]
    whole_high, whole_low, back_high, back_low, swapped_high, swapped_low, whole, sems = refs[pieces + 2 :]

    @pl.when(pl.program_id(0) == 0)
    def _():
        assemble(offsets_ref, piece_refs, whole, sems, whole_high, whole_low)

    section = dot3(split(rows_ref[...]), (whole_high[...], whole_low[...]), NN)
    swapped_high, swapped_low = chunk_of(swapped_high), chunk_of(swapped_low)
    swap_into(section, swapped_high, swapped_low)
    mixed = dot3(split(site_ref[...]), (swapped_high[...], swapped_low[...]), NN)
    unswap_into(mixed, chunk_of(back_high), chunk_of(back_low))


def block_of(ref):
    return ref.at[pl.ds(pl.multiple_of(pl.program_id(1) * WIDTH, WIDTH), WIDTH)]


def place(terms, sources_ref, staged, ahead_ref, behind_ref, kept_ref):
    for a in range(16):
        staged[:, a, :] = terms[16 * a : 16 * a + 16, :]
    slot = 0
    for ref in (ahead_ref, behind_ref, kept_ref):
        for block in range(ref.shape[0]):
            ref[block] = staged[pl.ds(sources_ref[slot] * 2, 2)]
            slot += 1


def edge_kernel(pieces, offsets_ref, sources_ref, *refs):
    piece_refs = refs[:pieces]
    back_high_ref, back_low_ref = refs[pieces : pieces + 2]
    whole_high, whole_low, ahead_ref, behind_ref, kept_ref, whole, staged, sems = refs[pieces + 2 :]

    @pl.when((pl.program_id(0) == 0) & (pl.program_id(1) == 0))
    def _():
        assemble(offsets_ref, piece_refs, whole, sems, whole_high, whole_low)

    rows = chunk_of(back_high_ref)[...], chunk_of(back_low_ref)[...]
    terms = dot3(rows, (block_of(whole_high)[...], block_of(whole_low)[...]), NT)
    place(terms, sources_ref, staged, ahead_ref, behind_ref, kept_ref)


def first_kernel(
    edge_ref,
    right_high_ref,
    right_low_ref,
    site_matrix_ref,
    swapped_high_ref,
    swapped_low_ref,
    second_high_ref,
    second_low_ref,
    site_ref,
    first_high,
    first_low,
):
    first = dot3(split(edge_ref[...]), (right_high_ref[...], right_low_ref[...]), NN)
    swap_into(first, first_high, first_low)
    mixed = dot3(split(site_matrix_ref[...]), (first_high[...], first_low[...]), TN)
    unswap_into(mixed, chunk_of(second_high_ref), chunk_of(second_low_ref))
    swapped = chunk_of(swapped_high_ref)[...], chunk_of(swapped_low_ref)[...]
    site = dot3((first_high[...], first_low[...]), swapped, NT)

    @pl.when(pl.program_id(0) == 0)
    def _():
        site_ref[...] = site

    @pl.when(pl.program_id(0) > 0)
    def _():
        site_ref[...] += site


def left_kernel(
    sources_ref, second_high_ref, second_low_ref, high_ref, low_ref, ahead_ref, behind_ref, kept_ref, staged
):
    rows = chunk_of(second_high_ref)[...], chunk_of(second_low_ref)[...]
    terms = dot3(rows, (block_of(high_ref)[...], block_of(low_ref)[...]), NT)
    place(terms, sources_ref, staged, ahead_ref, behind_ref, kept_ref)


def right_kernel(places_ref, back_high_ref, back_low_ref, edge_ref, own_ref, other_ref, turned_high, turned_low, placed):
    @pl.when(pl.program_id(0) == 0)
    def _():
        def turn(chunk, carry):
            rows = pl.ds(pl.multiple_of(chunk * ROWS, ROWS), ROWS)
            turned_high[:, rows] = back_high_ref[rows, :].T
            turned_low[:, rows] = back_low_ref[rows, :].T
            return carry

        lax.fori_loop(0, CHUNKS, turn, 0)

    terms = dot3((turned_high[...], turned_low[...]), split(edge_ref[...]), NN)
    for block in range(16):
        start = pl.multiple_of(places_ref[block], 64)
        placed[pl.ds(start, 64), :] = terms[64 * block : 64 * block + 64, :]
    own_ref[...] = placed[:512, :]
    other_ref[...] = placed[512:, :]


def resident(shape):
    return pl.BlockSpec(shape, lambda *_: (0,) * len(shape))


OUTSIDE = pl.BlockSpec(memory_space=pltpu.HBM)
HELD = pl.BlockSpec(memory_space=pltpu.VMEM)
SQUARE = jax.ShapeDtypeStruct((1024, 1024), BF16)
CHUNK = pl.BlockSpec((ROWS, 1024), lambda i, *_: (i, 0))


def back_call(offsets, pieces, rows, site_matrix):
    return pl.pallas_call(
        functools.partial(back_kernel, len(pieces)),
        out_shape=(SQUARE,) * 6,
        grid_spec=pltpu.PrefetchScalarGridSpec(
            num_scalar_prefetch=1,
            grid=(CHUNKS,),
            in_specs=[OUTSIDE] * len(pieces) + [CHUNK, resident((256, 256))],
            out_specs=[HELD] * 6,
            scratch_shapes=[pltpu.VMEM((1024, 1024), F32), pltpu.SemaphoreType.DMA((16,))],
        ),
        compiler_params=PARAMS,
        name="back",
    )(offsets, *pieces, rows, site_matrix)


BLOCKS = tuple(jax.ShapeDtypeStruct((count, 2, 64, 1024), F32) for count in (2, 2, 4))
BLOCK_SPECS = [pl.BlockSpec((count, 2, 16, WIDTH), lambda i, j, *_: (0, 0, i, j)) for count in (2, 2, 4)]


def edge_call(offsets, sources, pieces, back_split):
    return pl.pallas_call(
        functools.partial(edge_kernel, len(pieces)),
        out_shape=(SQUARE, SQUARE, *BLOCKS),
        grid_spec=pltpu.PrefetchScalarGridSpec(
            num_scalar_prefetch=2,
            grid=(CHUNKS, 1024 // WIDTH),
            in_specs=[OUTSIDE] * len(pieces) + [HELD, HELD],
            out_specs=[HELD] * 2 + BLOCK_SPECS,
            scratch_shapes=[
                pltpu.VMEM((1024, 1024), F32),
                pltpu.VMEM((16, 16, WIDTH), F32),
                pltpu.SemaphoreType.DMA((16,)),
            ],
        ),
        compiler_params=PARAMS,
        name="edge",
    )(offsets, sources, *pieces, *back_split)


def first_call(edge_rows, right_split, site_matrix, swapped_split):
    return pl.pallas_call(
        first_kernel,
        out_shape=(SQUARE, SQUARE, jax.ShapeDtypeStruct((256, 256), F32)),
        grid=(CHUNKS,),
        in_specs=[CHUNK] + [HELD] * 2 + [resident((256, 256))] + [HELD] * 2,
        out_specs=[HELD, HELD, resident((256, 256))],
        scratch_shapes=[pltpu.VMEM((ROWS, 1024), BF16)] * 2,
        compiler_params=PARAMS,
        name="first",
    )(edge_rows, *right_split, site_matrix, *swapped_split)


def left_call(sources, second_split, cotangent_split):
    return pl.pallas_call(
        left_kernel,
        out_shape=BLOCKS,
        grid_spec=pltpu.PrefetchScalarGridSpec(
            num_scalar_prefetch=1,
            grid=(CHUNKS, 1024 // WIDTH),
            in_specs=[HELD] * 4,
            out_specs=BLOCK_SPECS,
            scratch_shapes=[pltpu.VMEM((16, 16, WIDTH), F32)],
        ),
        compiler_params=PARAMS,
        name="left",
    )(sources, *second_split, *cotangent_split)


def right_call(places, back_split, edge_rows):
    column = lambda rows: pl.BlockSpec((rows, 256), lambda i, *_: (0, i))
    return pl.pallas_call(
        right_kernel,
        out_shape=(jax.ShapeDtypeStruct((512, 1024), F32),) * 2,
        grid_spec=pltpu.PrefetchScalarGridSpec(
            num_scalar_prefetch=1,
            grid=(4,),
            in_specs=[HELD] * 2 + [column(1024)],
            out_specs=[column(512)] * 2,
            scratch_shapes=[pltpu.VMEM((1024, 1024), BF16)] * 2 + [pltpu.VMEM((1024, 256), F32)],
        ),
        compiler_params=PARAMS,
        name="right",
    )(places, *back_split, edge_rows)


def row_permute(value, z, y, core):
    pairs = []
    for source in range(16):
        there = ((source // 8) ^ z) * 8 + ((source // 2 + y) % 4) * 2 + ((source % 2) ^ core)
        pairs.append((source, there))
    return lax.ppermute(value, "row", pairs)


def col_permute(value, z, x):
    return lax.ppermute(value, "col", [(i, ((i // 4) ^ z) * 4 + (i + x) % 4) for i in range(8)])


def col_reduce(ahead, behind, kept):
    from_behind = col_permute(ahead, 0, 1)
    from_ahead = col_permute(behind, 0, 3)
    far_behind = col_permute(kept[0] + from_behind[0], 0, 1)
    far_ahead = col_permute(kept[1] + from_ahead[0], 0, 3)
    other = kept[3] + from_behind[1] + far_ahead
    same = kept[2] + from_ahead[1] + far_behind
    return jnp.transpose(same + col_permute(other, 1, 0), (1, 0, 2))


def dense(value):
    cols, bond, width = value.shape
    return jnp.transpose(value.reshape(cols, 2, 8, width), (3, 2, 1, 0)).reshape(width, bond * cols)


def take(value, index):
    return lax.dynamic_index_in_dim(value, index, 0, keepdims=False, allow_negative_indices=False)


def on_device(edge_tensor, site_tensor, left_isometry, right_isometry, cotangent):
    row = lax.axis_index("row").astype(jnp.int32)
    col = lax.axis_index("col").astype(jnp.int32)
    z, y, core = row >> 3, (row >> 1) & 3, row & 1
    edge_rows = edge_tensor.reshape(1024, 1024)
    left_rows = pltpu.with_memory_space_constraint(left_isometry.reshape(1024, 1024), pltpu.HBM)

    def offset_of(other_z, steps, other_core):
        other_z, steps, other_core = (np.array(list(v), np.int32) for v in (other_z, steps, other_core))
        return ((z ^ other_z) * 8 + ((y - steps) & 3) * 2 + (core ^ other_core)) * 64

    site_matrix = jnp.transpose(site_tensor, (2, 1, 3, 0)).reshape(256, 256)
    order = [(j, steps, c) for c in (0, 1) for j in (0, 1) for steps in (0, 1, 3, 2)]
    cotangent_offsets = offset_of(*zip(*order))
    order = [(j, steps, c) for c in (0, 1) for steps in (0, 1, 3, 2) for j in (0, 1)]
    isometry_offsets = offset_of(*zip(*order))
    steps = np.array([2, 1, 2, 3, 1, 3, 0, 0], np.int32)
    others = np.array([0, 1, 1, 0, 0, 1, 0, 1], np.int32)
    sources = ((col >> 2) ^ others) * 4 + ((col + steps) & 3)
    blocks = np.array([(i % 2) * 8 + i // 2 for i in range(16)], np.int32)
    places = (((blocks & 1) ^ core) * 8 + (((blocks >> 1) - y) & 3) * 2 + ((blocks >> 3) ^ z)) * 64
    corners = [(core * 2 + z) ^ k for k in range(4)]
    ahead = [(y + k) & 3 for k in range(4)]
    first_row, at_low_z, at_low_core = ((4 - y) & 3) * 16, z == 0, core == 0

    early = dense(cotangent)
    early, right_isometry = lax.optimization_barrier((early, right_isometry))
    other = row_permute(early, 1, 0, 0)
    nearest = [row_permute(early, 0, steps, 0) for steps in (1, 3, 2)]
    values = (cotangent_offsets, isometry_offsets, sources, places)
    indices = (*corners, *ahead, first_row, at_low_z, at_low_core)
    other, values, indices = lax.optimization_barrier((other, values, indices))
    cotangent_offsets, isometry_offsets, sources, places = values
    corners, ahead, (first_row, at_low_z, at_low_core) = indices[:4], indices[4:8], indices[8:]
    own = dense(right_isometry)
    pair = jnp.concatenate([own, row_permute(own, 1, 0, 0)], 0)
    pieces = [early, *nearest, other, *(row_permute(other, 0, steps, 0) for steps in (1, 3, 2))]
    pairs = [pair] + [row_permute(pair, 0, steps, 0) for steps in (1, 3, 2)]

    pieces[3], site_matrix = lax.optimization_barrier((pieces[3], site_matrix))
    pieces += [row_permute(piece, 0, 0, 1) for piece in pieces]
    cotangent_high, cotangent_low, *rest = back_call(cotangent_offsets, pieces, left_rows, site_matrix)
    back_split, swapped_split = rest[:2], rest[2:]

    pairs += [row_permute(piece, 0, 0, 1) for piece in pairs]
    right_high, right_low, *edge_terms = edge_call(isometry_offsets, sources, pairs, back_split)
    edge_gradient = col_reduce(*edge_terms)
    *second_split, site_terms = first_call(edge_rows, (right_high, right_low), site_matrix, swapped_split)
    left_terms = left_call(sources, second_split, (cotangent_high, cotangent_low))
    left_gradient = col_reduce(*left_terms)

    right_own, right_other = right_call(places, back_split, edge_rows)

    part = site_terms.reshape(4, 64, 256)
    sends = [row_permute(take(part, corners[k]), k & 1, 0, k >> 1) for k in (1, 2, 3)]
    part = take(part, corners[0]) + sum(sends)
    part = part.reshape(4, 16, 256)
    part = take(part, ahead[0]) + sum(row_permute(take(part, ahead[k]), 0, k, 0) for k in (1, 2, 3))
    part = part + sum(col_permute(part, 0, k) for k in (1, 2, 3))
    part = part + col_permute(part, 1, 0)
    ring = [part] + [row_permute(part, 0, k, 0) for k in (3, 2, 1)]
    ring = jnp.concatenate(ring + ring, 0)
    part = lax.dynamic_slice(ring, (first_row, 0), (64, 256), allow_negative_indices=False)
    near, across, far = (row_permute(part, k & 1, 0, k >> 1) for k in (1, 2, 3))
    low = jnp.where(at_low_z, jnp.concatenate([part, near], 0), jnp.concatenate([near, part], 0))
    high = jnp.where(at_low_z, jnp.concatenate([across, far], 0), jnp.concatenate([far, across], 0))
    part = jnp.where(at_low_core, jnp.concatenate([low, high], 0), jnp.concatenate([high, low], 0))
    site_gradient = jnp.transpose(part.reshape(16, 16, 16, 16), (3, 1, 0, 2))

    right_own = right_own.reshape(4, 2, 64, 1024)
    received = row_permute(right_other, 0, 0, 1).reshape(4, 2, 64, 1024)
    total = [right_own[k] + received[k] for k in range(4)]
    total = total[0] + sum(row_permute(total[k], 0, k, 0) for k in (1, 3, 2))
    right_gradient = total[0] + row_permute(total[1], 1, 0, 0)

    return (
        edge_gradient,
        site_gradient,
        left_gradient,
        right_gradient.reshape(64, 1, 1024),
    )


def solution(mesh):
    in_specs = (
        P("row", None, None),
        P(),
        P("row", None, None),
        P("col", None, "row"),
        P("col", None, "row"),
    )
    out_specs = (P("row", "col", None), P(), P("row", "col", None), P("col", "row", None))

    return jax.shard_map(on_device, mesh=mesh, in_specs=in_specs, out_specs=out_specs, check_vma=False)
```

```python
import functools

import jax
import jax.numpy as jnp
import numpy as np
from jax import lax
from jax.experimental import pallas as pl
from jax.experimental.pallas import tpu as pltpu
from jax.sharding import PartitionSpec as P

F32, BF16 = jnp.float32, jnp.bfloat16
NN = (((1,), (0,)), ((), ()))
NT = (((1,), (1,)), ((), ()))
TN = (((0,), (0,)), ((), ()))
PARAMS = pltpu.CompilerParams(vmem_limit_bytes=16 << 20)
ROWS = 256
CHUNKS = 4
WIDTH = 512


def split(value):
    high = value.astype(BF16)
    return high, (value - high.astype(F32)).astype(BF16)


def dot3(left, right, dims):
    dot = functools.partial(lax.dot_general, dimension_numbers=dims, preferred_element_type=F32)
    return dot(left[0], right[0]) + (dot(left[0], right[1]) + dot(left[1], right[0]))


def swap_into(value, high_ref, low_ref):
    lane = lax.broadcasted_iota(jnp.int32, (16, 128), 1)
    for pair in range(8):
        for tile in range(8):
            first = value[32 * pair : 32 * pair + 16, 128 * tile : 128 * tile + 128]
            second = value[32 * pair + 16 : 32 * pair + 32, 128 * tile : 128 * tile + 128]
            even = jnp.where(lane < 64, first, pltpu.roll(second, 64, 1))
            odd = jnp.where(lane < 64, pltpu.roll(first, 64, 1), second)
            columns = slice(128 * pair, 128 * pair + 128)
            for start, part in ((16 * tile, even), (128 + 16 * tile, odd)):
                high, low = split(part)
                high_ref[start : start + 16, columns] = high
                low_ref[start : start + 16, columns] = low


def unswap_into(value, high_ref, low_ref):
    lane = lax.broadcasted_iota(jnp.int32, (16, 128), 1)
    for pair in range(8):
        for tile in range(8):
            columns = slice(128 * pair, 128 * pair + 128)
            even = value[16 * tile : 16 * tile + 16, columns]
            odd = value[128 + 16 * tile : 128 + 16 * tile + 16, columns]
            first = jnp.where(lane < 64, even, pltpu.roll(odd, 64, 1))
            second = jnp.where(lane < 64, pltpu.roll(even, 64, 1), odd)
            columns = slice(128 * tile, 128 * tile + 128)
            for start, part in ((32 * pair, first), (32 * pair + 16, second)):
                high, low = split(part)
                high_ref[start : start + 16, columns] = high
                low_ref[start : start + 16, columns] = low


def assemble(offsets_ref, piece_refs, whole_ref, sems, high_ref, low_ref):
    block = 64
    copies = []
    count = 0
    for piece in piece_refs:
        for part in range(piece.shape[0] // block):
            start = pl.multiple_of(offsets_ref[count], block)
            target = whole_ref.at[pl.ds(start, block)]
            copies.append((pltpu.make_async_copy(piece.at[pl.ds(part * block, block)], target, sems.at[count]), start))
            count += 1
    for copy, _ in copies:
        copy.start()
    for copy, start in copies:
        copy.wait()

        def some(index, carry, start=start):
            rows = pl.ds(pl.multiple_of(start + index * 16, 16), 16)
            high, low = split(whole_ref[rows, :])
            high_ref[rows, :] = high
            low_ref[rows, :] = low
            return carry

        lax.fori_loop(0, block // 16, some, 0)


def chunk_of(ref):
    return ref.at[pl.ds(pl.multiple_of(pl.program_id(0) * ROWS, ROWS), ROWS)]


def back_kernel(pieces, offsets_ref, *refs):
    piece_refs = refs[:pieces]
    rows_ref, site_ref = refs[pieces : pieces + 2]
    whole_high, whole_low, back_high, back_low, swapped_high, swapped_low, whole, sems = refs[pieces + 2 :]

    @pl.when(pl.program_id(0) == 0)
    def _():
        assemble(offsets_ref, piece_refs, whole, sems, whole_high, whole_low)

    section = dot3(split(rows_ref[...]), (whole_high[...], whole_low[...]), NN)
    swapped_high, swapped_low = chunk_of(swapped_high), chunk_of(swapped_low)
    swap_into(section, swapped_high, swapped_low)
    mixed = dot3(split(site_ref[...]), (swapped_high[...], swapped_low[...]), NN)
    unswap_into(mixed, chunk_of(back_high), chunk_of(back_low))


def block_of(ref):
    return ref.at[pl.ds(pl.multiple_of(pl.program_id(1) * WIDTH, WIDTH), WIDTH)]


def place(terms, sources_ref, staged, ahead_ref, behind_ref, kept_ref):
    for a in range(16):
        staged[:, a, :] = terms[16 * a : 16 * a + 16, :]
    slot = 0
    for ref in (ahead_ref, behind_ref, kept_ref):
        for block in range(ref.shape[0]):
            ref[block] = staged[pl.ds(sources_ref[slot] * 2, 2)]
            slot += 1


def edge_kernel(pieces, offsets_ref, sources_ref, *refs):
    piece_refs = refs[:pieces]
    back_high_ref, back_low_ref = refs[pieces : pieces + 2]
    whole_high, whole_low, ahead_ref, behind_ref, kept_ref, whole, staged, sems = refs[pieces + 2 :]

    @pl.when((pl.program_id(0) == 0) & (pl.program_id(1) == 0))
    def _():
        assemble(offsets_ref, piece_refs, whole, sems, whole_high, whole_low)

    rows = chunk_of(back_high_ref)[...], chunk_of(back_low_ref)[...]
    terms = dot3(rows, (block_of(whole_high)[...], block_of(whole_low)[...]), NT)
    place(terms, sources_ref, staged, ahead_ref, behind_ref, kept_ref)


def first_kernel(
    edge_ref,
    right_high_ref,
    right_low_ref,
    site_matrix_ref,
    swapped_high_ref,
    swapped_low_ref,
    second_high_ref,
    second_low_ref,
    site_ref,
    first_high,
    first_low,
):
    first = dot3(split(edge_ref[...]), (right_high_ref[...], right_low_ref[...]), NN)
    swap_into(first, first_high, first_low)
    mixed = dot3(split(site_matrix_ref[...]), (first_high[...], first_low[...]), TN)
    unswap_into(mixed, chunk_of(second_high_ref), chunk_of(second_low_ref))
    swapped = chunk_of(swapped_high_ref)[...], chunk_of(swapped_low_ref)[...]
    site = dot3((first_high[...], first_low[...]), swapped, NT)

    @pl.when(pl.program_id(0) == 0)
    def _():
        site_ref[...] = site

    @pl.when(pl.program_id(0) > 0)
    def _():
        site_ref[...] += site


def left_kernel(
    sources_ref, second_high_ref, second_low_ref, high_ref, low_ref, ahead_ref, behind_ref, kept_ref, staged
):
    rows = chunk_of(second_high_ref)[...], chunk_of(second_low_ref)[...]
    terms = dot3(rows, (block_of(high_ref)[...], block_of(low_ref)[...]), NT)
    place(terms, sources_ref, staged, ahead_ref, behind_ref, kept_ref)


def right_kernel(places_ref, back_high_ref, back_low_ref, edge_ref, own_ref, other_ref, turned_high, turned_low, placed):
    @pl.when(pl.program_id(0) == 0)
    def _():
        def turn(chunk, carry):
            rows = pl.ds(pl.multiple_of(chunk * ROWS, ROWS), ROWS)
            turned_high[:, rows] = back_high_ref[rows, :].T
            turned_low[:, rows] = back_low_ref[rows, :].T
            return carry

        lax.fori_loop(0, CHUNKS, turn, 0)

    terms = dot3((turned_high[...], turned_low[...]), split(edge_ref[...]), NN)
    for block in range(16):
        start = pl.multiple_of(places_ref[block], 64)
        placed[pl.ds(start, 64), :] = terms[64 * block : 64 * block + 64, :]
    own_ref[...] = placed[:512, :]
    other_ref[...] = placed[512:, :]


def resident(shape):
    return pl.BlockSpec(shape, lambda *_: (0,) * len(shape))


OUTSIDE = pl.BlockSpec(memory_space=pltpu.HBM)
HELD = pl.BlockSpec(memory_space=pltpu.VMEM)
SQUARE = jax.ShapeDtypeStruct((1024, 1024), BF16)
CHUNK = pl.BlockSpec((ROWS, 1024), lambda i, *_: (i, 0))


def back_call(offsets, pieces, rows, site_matrix):
    return pl.pallas_call(
        functools.partial(back_kernel, len(pieces)),
        out_shape=(SQUARE,) * 6,
        grid_spec=pltpu.PrefetchScalarGridSpec(
            num_scalar_prefetch=1,
            grid=(CHUNKS,),
            in_specs=[OUTSIDE] * len(pieces) + [CHUNK, resident((256, 256))],
            out_specs=[HELD] * 6,
            scratch_shapes=[pltpu.VMEM((1024, 1024), F32), pltpu.SemaphoreType.DMA((16,))],
        ),
        compiler_params=PARAMS,
        name="back",
    )(offsets, *pieces, rows, site_matrix)


BLOCKS = tuple(jax.ShapeDtypeStruct((count, 2, 64, 1024), F32) for count in (2, 2, 4))
BLOCK_SPECS = [pl.BlockSpec((count, 2, 16, WIDTH), lambda i, j, *_: (0, 0, i, j)) for count in (2, 2, 4)]


def edge_call(offsets, sources, pieces, back_split):
    return pl.pallas_call(
        functools.partial(edge_kernel, len(pieces)),
        out_shape=(SQUARE, SQUARE, *BLOCKS),
        grid_spec=pltpu.PrefetchScalarGridSpec(
            num_scalar_prefetch=2,
            grid=(CHUNKS, 1024 // WIDTH),
            in_specs=[OUTSIDE] * len(pieces) + [HELD, HELD],
            out_specs=[HELD] * 2 + BLOCK_SPECS,
            scratch_shapes=[
                pltpu.VMEM((1024, 1024), F32),
                pltpu.VMEM((16, 16, WIDTH), F32),
                pltpu.SemaphoreType.DMA((16,)),
            ],
        ),
        compiler_params=PARAMS,
        name="edge",
    )(offsets, sources, *pieces, *back_split)


def first_call(edge_rows, right_split, site_matrix, swapped_split):
    return pl.pallas_call(
        first_kernel,
        out_shape=(SQUARE, SQUARE, jax.ShapeDtypeStruct((256, 256), F32)),
        grid=(CHUNKS,),
        in_specs=[CHUNK] + [HELD] * 2 + [resident((256, 256))] + [HELD] * 2,
        out_specs=[HELD, HELD, resident((256, 256))],
        scratch_shapes=[pltpu.VMEM((ROWS, 1024), BF16)] * 2,
        compiler_params=PARAMS,
        name="first",
    )(edge_rows, *right_split, site_matrix, *swapped_split)


def left_call(sources, second_split, cotangent_split):
    return pl.pallas_call(
        left_kernel,
        out_shape=BLOCKS,
        grid_spec=pltpu.PrefetchScalarGridSpec(
            num_scalar_prefetch=1,
            grid=(CHUNKS, 1024 // WIDTH),
            in_specs=[HELD] * 4,
            out_specs=BLOCK_SPECS,
            scratch_shapes=[pltpu.VMEM((16, 16, WIDTH), F32)],
        ),
        compiler_params=PARAMS,
        name="left",
    )(sources, *second_split, *cotangent_split)


def right_call(places, back_split, edge_rows):
    column = lambda rows: pl.BlockSpec((rows, 256), lambda i, *_: (0, i))
    return pl.pallas_call(
        right_kernel,
        out_shape=(jax.ShapeDtypeStruct((512, 1024), F32),) * 2,
        grid_spec=pltpu.PrefetchScalarGridSpec(
            num_scalar_prefetch=1,
            grid=(4,),
            in_specs=[HELD] * 2 + [column(1024)],
            out_specs=[column(512)] * 2,
            scratch_shapes=[pltpu.VMEM((1024, 1024), BF16)] * 2 + [pltpu.VMEM((1024, 256), F32)],
        ),
        compiler_params=PARAMS,
        name="right",
    )(places, *back_split, edge_rows)


def row_permute(value, z, y, core):
    pairs = []
    for source in range(16):
        there = ((source // 8) ^ z) * 8 + ((source // 2 + y) % 4) * 2 + ((source % 2) ^ core)
        pairs.append((source, there))
    return lax.ppermute(value, "row", pairs)


def col_permute(value, z, x):
    return lax.ppermute(value, "col", [(i, ((i // 4) ^ z) * 4 + (i + x) % 4) for i in range(8)])


def col_reduce(ahead, behind, kept):
    from_behind = col_permute(ahead, 0, 1)
    from_ahead = col_permute(behind, 0, 3)
    sums = kept[0] + from_behind[0], kept[1] + from_ahead[0]
    far_behind = col_permute(sums[0], 0, 1)
    far_ahead = col_permute(sums[1], 0, 3)
    other = kept[3] + from_behind[1] + far_ahead
    same = kept[2] + from_ahead[1] + far_behind
    return jnp.transpose(same + col_permute(other, 1, 0), (1, 0, 2))


def dense(value):
    cols, bond, width = value.shape
    return jnp.transpose(value.reshape(cols, 2, 8, width), (3, 2, 1, 0)).reshape(width, bond * cols)


def take(value, index):
    return lax.dynamic_index_in_dim(value, index, 0, keepdims=False, allow_negative_indices=False)


def on_device(edge_tensor, site_tensor, left_isometry, right_isometry, cotangent):
    row = lax.axis_index("row").astype(jnp.int32)
    col = lax.axis_index("col").astype(jnp.int32)
    z, y, core = row >> 3, (row >> 1) & 3, row & 1
    edge_rows = edge_tensor.reshape(1024, 1024)
    left_rows = pltpu.with_memory_space_constraint(left_isometry.reshape(1024, 1024), pltpu.HBM)

    def offset_of(other_z, steps, other_core):
        other_z, steps, other_core = (np.array(list(v), np.int32) for v in (other_z, steps, other_core))
        return ((z ^ other_z) * 8 + ((y - steps) & 3) * 2 + (core ^ other_core)) * 64

    site_matrix = jnp.transpose(site_tensor, (2, 1, 3, 0)).reshape(256, 256)
    order = [(j, steps, c) for c in (0, 1) for j in (0, 1) for steps in (0, 1, 3, 2)]
    cotangent_offsets = offset_of(*zip(*order))
    order = [(j, steps, c) for c in (0, 1) for steps in (0, 1, 3, 2) for j in (0, 1)]
    isometry_offsets = offset_of(*zip(*order))
    steps = np.array([2, 1, 2, 3, 1, 3, 0, 0], np.int32)
    others = np.array([0, 1, 1, 0, 0, 1, 0, 1], np.int32)
    sources = ((col >> 2) ^ others) * 4 + ((col + steps) & 3)
    blocks = np.array([(i % 2) * 8 + i // 2 for i in range(16)], np.int32)
    places = (((blocks & 1) ^ core) * 8 + (((blocks >> 1) - y) & 3) * 2 + ((blocks >> 3) ^ z)) * 64
    cores, sides = [core, core ^ 1], [z, z ^ 1]
    ahead = [(y + k) & 3 for k in range(4)]
    first_row, at_low_z, at_low_core = ((4 - y) & 3) * 32, z == 0, core == 0

    early = dense(cotangent)
    early, right_isometry = lax.optimization_barrier((early, right_isometry))
    other = row_permute(early, 1, 0, 0)
    nearest = [row_permute(early, 0, steps, 0) for steps in (1, 3, 2)]
    values = (cotangent_offsets, isometry_offsets, sources, places)
    indices = (*cores, *sides, *ahead, first_row, at_low_z, at_low_core)
    other, values, indices = lax.optimization_barrier((other, values, indices))
    cotangent_offsets, isometry_offsets, sources, places = values
    cores, sides, ahead, (first_row, at_low_z, at_low_core) = indices[:2], indices[2:4], indices[4:8], indices[8:]
    own = dense(right_isometry)
    pair = jnp.concatenate([own, row_permute(own, 1, 0, 0)], 0)
    pieces = [early, *nearest, other, *(row_permute(other, 0, steps, 0) for steps in (1, 3, 2))]
    pairs = [pair] + [row_permute(pair, 0, steps, 0) for steps in (1, 3, 2)]

    pieces[3], site_matrix = lax.optimization_barrier((pieces[3], site_matrix))
    pieces += [row_permute(piece, 0, 0, 1) for piece in pieces]
    cotangent_high, cotangent_low, *rest = back_call(cotangent_offsets, pieces, left_rows, site_matrix)
    back_split, swapped_split = rest[:2], rest[2:]

    pairs += [row_permute(piece, 0, 0, 1) for piece in pairs]
    right_high, right_low, *edge_terms = edge_call(isometry_offsets, sources, pairs, back_split)
    edge_gradient = col_reduce(*edge_terms)
    *second_split, site_terms = first_call(edge_rows, (right_high, right_low), site_matrix, swapped_split)
    left_terms = left_call(sources, second_split, (cotangent_high, cotangent_low))
    left_gradient = col_reduce(*left_terms)

    right_own, right_other = right_call(places, back_split, edge_rows)

    part = site_terms.reshape(2, 4, 2, 16, 256)

    def corner(k):
        start = (cores[k >> 1], 0, sides[k & 1], 0, 0)
        return lax.dynamic_slice(part, start, (1, 4, 1, 16, 256), allow_negative_indices=False).reshape(64, 256)

    part = corner(0) + sum(row_permute(corner(k), k & 1, 0, k >> 1) for k in (1, 2, 3))
    part = part.reshape(4, 16, 256)
    part = take(part, ahead[0]) + sum(row_permute(take(part, ahead[k]), 0, k, 0) for k in (1, 2, 3))
    part = part + col_permute(part, 1, 0)
    part = part + sum(col_permute(part, 0, k) for k in (1, 2, 3))
    other = row_permute(part, 1, 0, 0)
    part = jnp.where(at_low_z, jnp.concatenate([part, other], 0), jnp.concatenate([other, part], 0))
    ring = [part] + [row_permute(part, 0, k, 0) for k in (3, 2, 1)]
    ring = jnp.concatenate(ring + ring, 0)
    part = lax.dynamic_slice(ring, (first_row, 0), (128, 256), allow_negative_indices=False)
    other = row_permute(part, 0, 0, 1)
    part = jnp.where(at_low_core, jnp.concatenate([part, other], 0), jnp.concatenate([other, part], 0))
    site_gradient = jnp.transpose(part.reshape(16, 16, 16, 16), (3, 1, 0, 2))

    right_own = right_own.reshape(4, 2, 64, 1024)
    received = row_permute(right_other, 0, 0, 1).reshape(4, 2, 64, 1024)
    total = [right_own[k] + received[k] for k in range(4)]
    total = total[0] + sum(row_permute(total[k], 0, k, 0) for k in (1, 3, 2))
    right_gradient = total[0] + row_permute(total[1], 1, 0, 0)

    return (
        edge_gradient,
        site_gradient,
        left_gradient,
        right_gradient.reshape(64, 1, 1024),
    )


def solution(mesh):
    in_specs = (
        P("row", None, None),
        P(),
        P("row", None, None),
        P("col", None, "row"),
        P("col", None, "row"),
    )
    out_specs = (P("row", "col", None), P(), P("row", "col", None), P("col", "row", None))

    return jax.shard_map(on_device, mesh=mesh, in_specs=in_specs, out_specs=out_specs, check_vma=False)
```

```python
import functools

import jax
import jax.numpy as jnp
import numpy as np
from jax import lax
from jax.experimental import pallas as pl
from jax.experimental.pallas import tpu as pltpu
from jax.sharding import PartitionSpec as P

F32, BF16 = jnp.float32, jnp.bfloat16
NN = (((1,), (0,)), ((), ()))
NT = (((1,), (1,)), ((), ()))
TN = (((0,), (0,)), ((), ()))
PARAMS = pltpu.CompilerParams(vmem_limit_bytes=16 << 20)
ROWS = 256
CHUNKS = 4
WIDTH = 256


def split(value):
    high = value.astype(BF16)
    return high, (value - high.astype(F32)).astype(BF16)


def dot3(left, right, dims):
    dot = functools.partial(lax.dot_general, dimension_numbers=dims, preferred_element_type=F32)
    return dot(left[0], right[0]) + (dot(left[0], right[1]) + dot(left[1], right[0]))


def swap_into(value, high_ref, low_ref):
    lane = lax.broadcasted_iota(jnp.int32, (16, 128), 1)
    for pair in range(8):
        for tile in range(8):
            first = value[32 * pair : 32 * pair + 16, 128 * tile : 128 * tile + 128]
            second = value[32 * pair + 16 : 32 * pair + 32, 128 * tile : 128 * tile + 128]
            even = jnp.where(lane < 64, first, pltpu.roll(second, 64, 1))
            odd = jnp.where(lane < 64, pltpu.roll(first, 64, 1), second)
            columns = slice(128 * pair, 128 * pair + 128)
            for start, part in ((16 * tile, even), (128 + 16 * tile, odd)):
                high, low = split(part)
                high_ref[start : start + 16, columns] = high
                low_ref[start : start + 16, columns] = low


def unswap_into(value, high_ref, low_ref):
    lane = lax.broadcasted_iota(jnp.int32, (16, 128), 1)
    for pair in range(8):
        for tile in range(8):
            columns = slice(128 * pair, 128 * pair + 128)
            even = value[16 * tile : 16 * tile + 16, columns]
            odd = value[128 + 16 * tile : 128 + 16 * tile + 16, columns]
            first = jnp.where(lane < 64, even, pltpu.roll(odd, 64, 1))
            second = jnp.where(lane < 64, pltpu.roll(even, 64, 1), odd)
            columns = slice(128 * tile, 128 * tile + 128)
            for start, part in ((32 * pair, first), (32 * pair + 16, second)):
                high, low = split(part)
                high_ref[start : start + 16, columns] = high
                low_ref[start : start + 16, columns] = low


def assemble(offsets_ref, piece_refs, whole_ref, sems, high_ref, low_ref):
    block = 64
    copies = []
    count = 0
    for piece in piece_refs:
        for part in range(piece.shape[0] // block):
            start = pl.multiple_of(offsets_ref[count], block)
            target = whole_ref.at[pl.ds(start, block)]
            copies.append(pltpu.make_async_copy(piece.at[pl.ds(part * block, block)], target, sems.at[count]))
            count += 1
    for copy in copies:
        copy.start()
    for group in range(4):
        for copy in copies[4 * group : 4 * group + 4]:
            copy.wait()

        def some(index, carry, group=group):
            start = offsets_ref[4 * group + (index >> 2)] + (index & 3) * 16
            rows = pl.ds(pl.multiple_of(start, 16), 16)
            high, low = split(whole_ref[rows, :])
            high_ref[rows, :] = high
            low_ref[rows, :] = low
            return carry

        lax.fori_loop(0, 16, some, 0)


def chunk_of(ref):
    return ref.at[pl.ds(pl.multiple_of(pl.program_id(0) * ROWS, ROWS), ROWS)]


def back_kernel(pieces, offsets_ref, *refs):
    piece_refs = refs[:pieces]
    rows_ref, site_ref = refs[pieces : pieces + 2]
    whole_high, whole_low, back_high, back_low, swapped_high, swapped_low, whole, sems = refs[pieces + 2 :]

    @pl.when(pl.program_id(0) == 0)
    def _():
        assemble(offsets_ref, piece_refs, whole, sems, whole_high, whole_low)

    section = dot3(split(rows_ref[...]), (whole_high[...], whole_low[...]), NN)
    swapped_high, swapped_low = chunk_of(swapped_high), chunk_of(swapped_low)
    swap_into(section, swapped_high, swapped_low)
    mixed = dot3(split(site_ref[...]), (swapped_high[...], swapped_low[...]), NN)
    unswap_into(mixed, chunk_of(back_high), chunk_of(back_low))


def block_of(ref):
    return ref.at[pl.ds(pl.multiple_of(pl.program_id(1) * WIDTH, WIDTH), WIDTH)]


def place(terms, sources_ref, staged, out_refs):
    for a in range(16):
        staged[:, a, :] = terms[16 * a : 16 * a + 16, :]
    slot = 0
    for ref in out_refs:
        for unit in range(ref.shape[0]):
            ref[unit] = staged[sources_ref[slot]]
            slot += 1


def edge_kernel(pieces, offsets_ref, sources_ref, *refs):
    piece_refs = refs[:pieces]
    back_high_ref, back_low_ref = refs[pieces : pieces + 2]
    whole_high, whole_low, *out_refs, whole, staged, sems = refs[pieces + 2 :]

    @pl.when((pl.program_id(0) == 0) & (pl.program_id(1) == 0))
    def _():
        assemble(offsets_ref, piece_refs, whole, sems, whole_high, whole_low)

    rows = chunk_of(back_high_ref)[...], chunk_of(back_low_ref)[...]
    terms = dot3(rows, (block_of(whole_high)[...], block_of(whole_low)[...]), NT)
    place(terms, sources_ref, staged, out_refs)


def first_kernel(
    edge_ref,
    right_high_ref,
    right_low_ref,
    site_matrix_ref,
    swapped_high_ref,
    swapped_low_ref,
    second_high_ref,
    second_low_ref,
    site_ref,
    first_high,
    first_low,
):
    first = dot3(split(edge_ref[...]), (right_high_ref[...], right_low_ref[...]), NN)
    swap_into(first, first_high, first_low)
    mixed = dot3(split(site_matrix_ref[...]), (first_high[...], first_low[...]), TN)
    unswap_into(mixed, chunk_of(second_high_ref), chunk_of(second_low_ref))
    swapped = chunk_of(swapped_high_ref)[...], chunk_of(swapped_low_ref)[...]
    site = dot3((first_high[...], first_low[...]), swapped, NT)

    @pl.when(pl.program_id(0) == 0)
    def _():
        site_ref[...] = site

    @pl.when(pl.program_id(0) > 0)
    def _():
        site_ref[...] += site


def left_kernel(sources_ref, second_high_ref, second_low_ref, high_ref, low_ref, *refs):
    *out_refs, staged = refs
    rows = chunk_of(second_high_ref)[...], chunk_of(second_low_ref)[...]
    terms = dot3(rows, (block_of(high_ref)[...], block_of(low_ref)[...]), NT)
    place(terms, sources_ref, staged, out_refs)


def right_kernel(places_ref, back_high_ref, back_low_ref, edge_ref, own_ref, other_ref, turned_high, turned_low, placed):
    half = pl.program_id(1)

    @pl.when((pl.program_id(0) == 0) & (half == 0))
    def _():
        def turn(chunk, carry):
            rows = pl.ds(pl.multiple_of(chunk * ROWS, ROWS), ROWS)
            turned_high[:, rows] = back_high_ref[rows, :].T
            turned_low[:, rows] = back_low_ref[rows, :].T
            return carry

        lax.fori_loop(0, CHUNKS, turn, 0)

    rows = pl.ds(pl.multiple_of(half * 512, 512), 512)
    terms = dot3((turned_high[rows, :], turned_low[rows, :]), split(edge_ref[...]), NN)
    for block in range(8):
        start = pl.multiple_of(places_ref[half * 8 + block], 64)
        placed[pl.ds(start, 64), :] = terms[64 * block : 64 * block + 64, :]

    @pl.when(half == 1)
    def _():
        own_ref[...] = placed[:512, :]
        other_ref[...] = placed[512:, :]


def resident(shape):
    return pl.BlockSpec(shape, lambda *_: (0,) * len(shape))


OUTSIDE = pl.BlockSpec(memory_space=pltpu.HBM)
HELD = pl.BlockSpec(memory_space=pltpu.VMEM)
SQUARE = jax.ShapeDtypeStruct((1024, 1024), BF16)
CHUNK = pl.BlockSpec((ROWS, 1024), lambda i, *_: (i, 0))


def back_call(offsets, pieces, rows, site_matrix):
    return pl.pallas_call(
        functools.partial(back_kernel, len(pieces)),
        out_shape=(SQUARE,) * 6,
        grid_spec=pltpu.PrefetchScalarGridSpec(
            num_scalar_prefetch=1,
            grid=(CHUNKS,),
            in_specs=[OUTSIDE] * len(pieces) + [CHUNK, resident((256, 256))],
            out_specs=[HELD] * 6,
            scratch_shapes=[pltpu.VMEM((1024, 1024), F32), pltpu.SemaphoreType.DMA((16,))],
        ),
        compiler_params=PARAMS,
        name="back",
    )(offsets, *pieces, rows, site_matrix)


def units(*counts):
    shapes = tuple(jax.ShapeDtypeStruct((count, 64, 1024), F32) for count in counts)
    return shapes, [pl.BlockSpec((count, 16, WIDTH), lambda i, j, *_: (0, i, j)) for count in counts]


EDGE_SHAPES, EDGE_SPECS = units(4, 4, 8)
LEFT_SHAPES, LEFT_SPECS = units(2, 2, 4, 2, 2, 4)


def edge_call(offsets, sources, pieces, back_split):
    return pl.pallas_call(
        functools.partial(edge_kernel, len(pieces)),
        out_shape=(SQUARE, SQUARE, *EDGE_SHAPES),
        grid_spec=pltpu.PrefetchScalarGridSpec(
            num_scalar_prefetch=2,
            grid=(CHUNKS, 1024 // WIDTH),
            in_specs=[OUTSIDE] * len(pieces) + [HELD, HELD],
            out_specs=[HELD] * 2 + EDGE_SPECS,
            scratch_shapes=[
                pltpu.VMEM((1024, 1024), F32),
                pltpu.VMEM((16, 16, WIDTH), F32),
                pltpu.SemaphoreType.DMA((16,)),
            ],
        ),
        compiler_params=PARAMS,
        name="edge",
    )(offsets, sources, *pieces, *back_split)


def first_call(edge_rows, right_split, site_matrix, swapped_split):
    return pl.pallas_call(
        first_kernel,
        out_shape=(SQUARE, SQUARE, jax.ShapeDtypeStruct((256, 256), F32)),
        grid=(CHUNKS,),
        in_specs=[CHUNK] + [HELD] * 2 + [resident((256, 256))] + [HELD] * 2,
        out_specs=[HELD, HELD, resident((256, 256))],
        scratch_shapes=[pltpu.VMEM((ROWS, 1024), BF16)] * 2,
        compiler_params=PARAMS,
        name="first",
    )(edge_rows, *right_split, site_matrix, *swapped_split)


def left_call(left_sources, second_split, cotangent_split):
    return pl.pallas_call(
        left_kernel,
        out_shape=LEFT_SHAPES,
        grid_spec=pltpu.PrefetchScalarGridSpec(
            num_scalar_prefetch=1,
            grid=(CHUNKS, 1024 // WIDTH),
            in_specs=[HELD] * 4,
            out_specs=LEFT_SPECS,
            scratch_shapes=[pltpu.VMEM((16, 16, WIDTH), F32)],
        ),
        compiler_params=PARAMS,
        name="left",
    )(left_sources, *second_split, *cotangent_split)


def right_call(places, back_split, edge_rows):
    column = lambda rows: pl.BlockSpec((rows, 256), lambda i, j, *_: (0, i))
    return pl.pallas_call(
        right_kernel,
        out_shape=(jax.ShapeDtypeStruct((512, 1024), F32),) * 2,
        grid_spec=pltpu.PrefetchScalarGridSpec(
            num_scalar_prefetch=1,
            grid=(4, 2),
            in_specs=[HELD] * 2 + [column(1024)],
            out_specs=[column(512)] * 2,
            scratch_shapes=[pltpu.VMEM((1024, 1024), BF16)] * 2 + [pltpu.VMEM((1024, 256), F32)],
        ),
        compiler_params=PARAMS,
        name="right",
    )(places, *back_split, edge_rows)


def row_permute(value, z, y, core):
    pairs = []
    for source in range(16):
        there = ((source // 8) ^ z) * 8 + ((source // 2 + y) % 4) * 2 + ((source % 2) ^ core)
        pairs.append((source, there))
    return lax.ppermute(value, "row", pairs)


def col_permute(value, z, x):
    return lax.ppermute(value, "col", [(i, ((i // 4) ^ z) * 4 + (i + x) % 4) for i in range(8)])


def ring_sum(ahead, behind, kept):
    from_behind = col_permute(ahead, 0, 1)
    from_ahead = col_permute(behind, 0, 3)
    sums = lax.optimization_barrier((kept[0] + from_behind[0], kept[1] + from_ahead[0]))
    far_behind = col_permute(sums[0], 0, 1)
    far_ahead = col_permute(sums[1], 0, 3)
    return kept[2] + from_ahead[1] + far_behind, kept[3] + from_behind[1] + far_ahead


def col_sources(col, steps, others, halves):
    steps, others, halves = (np.array(v, np.int32) for v in (steps, others, halves))
    return (((col >> 2) ^ others) * 4 + ((col + steps) & 3)) * 2 + halves


def dense(value):
    cols, bond, width = value.shape
    return jnp.transpose(value.reshape(cols, 2, 8, width), (3, 2, 1, 0)).reshape(width, bond * cols)


def take(value, index):
    return lax.dynamic_index_in_dim(value, index, 0, keepdims=False, allow_negative_indices=False)


def on_device(edge_tensor, site_tensor, left_isometry, right_isometry, cotangent):
    row = lax.axis_index("row").astype(jnp.int32)
    col = lax.axis_index("col").astype(jnp.int32)
    z, y, core = row >> 3, (row >> 1) & 3, row & 1
    edge_rows = edge_tensor.reshape(1024, 1024)
    left_rows = pltpu.with_memory_space_constraint(left_isometry.reshape(1024, 1024), pltpu.HBM)

    def offset_of(other_z, steps, other_core):
        other_z, steps, other_core = (np.array(list(v), np.int32) for v in (other_z, steps, other_core))
        return ((z ^ other_z) * 8 + ((y - steps) & 3) * 2 + (core ^ other_core)) * 64

    site_matrix = jnp.transpose(site_tensor, (2, 1, 3, 0)).reshape(256, 256)
    order = [(j, steps, c) for c in (0, 1) for j in (0, 1) for steps in (0, 1, 3, 2)]
    cotangent_offsets = offset_of(*zip(*order))
    order = [(j, steps, c) for c in (0, 1) for steps in (0, 1, 3, 2) for j in (0, 1)]
    isometry_offsets = offset_of(*zip(*order))
    order = (2, 1, 2, 3, 1, 3, 0, 0)
    halves = (0, 1, 1, 0, 0, 1, 0, 1)
    edge_sources = col_sources(col, np.repeat(order, 2), np.repeat(halves, 2), (0, 1) * 8)
    left_sources = col_sources(col, order * 2, (1,) * 8 + (0,) * 8, halves * 2)
    blocks = np.array([(i % 2) * 8 + i // 2 for i in range(16)], np.int32)
    places = (((blocks & 1) ^ core) * 8 + (((blocks >> 1) - y) & 3) * 2 + ((blocks >> 3) ^ z)) * 64
    cores, sides = [core, core ^ 1], [z, z ^ 1]
    ahead = [(y + k) & 3 for k in range(4)]
    first_row, at_low_z, at_low_core = ((4 - y) & 3) * 32, z == 0, core == 0

    early = dense(cotangent)
    early, right_isometry = lax.optimization_barrier((early, right_isometry))
    other = row_permute(early, 1, 0, 0)
    nearest = [row_permute(early, 0, steps, 0) for steps in (1, 3, 2)]
    values = (cotangent_offsets, isometry_offsets, edge_sources, left_sources, places)
    indices = (*cores, *sides, *ahead, first_row, at_low_z, at_low_core)
    other, values, indices = lax.optimization_barrier((other, values, indices))
    cotangent_offsets, isometry_offsets, edge_sources, left_sources, places = values
    cores, sides, ahead, (first_row, at_low_z, at_low_core) = indices[:2], indices[2:4], indices[4:8], indices[8:]
    own = dense(right_isometry)
    pair = jnp.concatenate([own, row_permute(own, 1, 0, 0)], 0)
    pieces = [early, *nearest, other, *(row_permute(other, 0, steps, 0) for steps in (1, 3, 2))]
    pairs = [pair] + [row_permute(pair, 0, steps, 0) for steps in (1, 3, 2)]

    pieces[3], site_matrix = lax.optimization_barrier((pieces[3], site_matrix))
    pieces += [row_permute(piece, 0, 0, 1) for piece in pieces]
    cotangent_high, cotangent_low, *rest = back_call(cotangent_offsets, pieces, left_rows, site_matrix)
    back_split, swapped_split = rest[:2], rest[2:]

    pairs += [row_permute(piece, 0, 0, 1) for piece in pairs]
    right_high, right_low, *edge_terms = edge_call(isometry_offsets, edge_sources, pairs, back_split)
    same, other = ring_sum(*(part.reshape(-1, 2, 64, 1024) for part in edge_terms))
    other = col_permute(other, 1, 0)
    edge_gradient = jnp.transpose(same + other, (1, 0, 2))
    *second_split, site_terms = first_call(edge_rows, (right_high, right_low), site_matrix, swapped_split)
    left_terms = left_call(left_sources, second_split, (cotangent_high, cotangent_low))
    other = jnp.stack(ring_sum(*left_terms[:3]))
    other = col_permute(other, 1, 0)
    left_gradient = jnp.transpose(jnp.stack(ring_sum(*left_terms[3:])) + other, (1, 0, 2))

    right_own, right_other = right_call(places, back_split, edge_rows)

    part = site_terms.reshape(2, 4, 2, 16, 256)

    def corner(k):
        start = (cores[k >> 1], 0, sides[k & 1], 0, 0)
        return lax.dynamic_slice(part, start, (1, 4, 1, 16, 256), allow_negative_indices=False).reshape(64, 256)

    part = corner(0) + sum(row_permute(corner(k), k & 1, 0, k >> 1) for k in (1, 2, 3))
    part = part.reshape(4, 16, 256)
    part = take(part, ahead[0]) + sum(row_permute(take(part, ahead[k]), 0, k, 0) for k in (1, 2, 3))
    part = part + col_permute(part, 1, 0)
    part = part + sum(col_permute(part, 0, k) for k in (1, 2, 3))
    other = row_permute(part, 1, 0, 0)
    part = jnp.where(at_low_z, jnp.concatenate([part, other], 0), jnp.concatenate([other, part], 0))
    ring = [part] + [row_permute(part, 0, k, 0) for k in (3, 2, 1)]
    ring = jnp.concatenate(ring + ring, 0)
    part = lax.dynamic_slice(ring, (first_row, 0), (128, 256), allow_negative_indices=False)
    other = row_permute(part, 0, 0, 1)
    part = jnp.where(at_low_core, jnp.concatenate([part, other], 0), jnp.concatenate([other, part], 0))
    site_gradient = jnp.transpose(part.reshape(16, 16, 16, 16), (3, 1, 0, 2))

    right_own = right_own.reshape(4, 2, 64, 1024)
    received = row_permute(right_other, 0, 0, 1).reshape(4, 2, 64, 1024)
    total = [right_own[k] + received[k] for k in range(4)]
    total = total[0] + sum(row_permute(total[k], 0, k, 0) for k in (1, 3, 2))
    right_gradient = total[0] + row_permute(total[1], 1, 0, 0)

    return (
        edge_gradient,
        site_gradient,
        left_gradient,
        right_gradient.reshape(64, 1, 1024),
    )


def solution(mesh):
    in_specs = (
        P("row", None, None),
        P(),
        P("row", None, None),
        P("col", None, "row"),
        P("col", None, "row"),
    )
    out_specs = (P("row", "col", None), P(), P("row", "col", None), P("col", "row", None))

    return jax.shard_map(on_device, mesh=mesh, in_specs=in_specs, out_specs=out_specs, check_vma=False)
```

```python
import functools

import jax
import jax.numpy as jnp
import numpy as np
from jax import lax
from jax.experimental import pallas as pl
from jax.experimental.pallas import tpu as pltpu
from jax.sharding import PartitionSpec as P

F32, BF16 = jnp.float32, jnp.bfloat16
NN = (((1,), (0,)), ((), ()))
NT = (((1,), (1,)), ((), ()))
TN = (((0,), (0,)), ((), ()))
PARAMS = pltpu.CompilerParams(vmem_limit_bytes=16 << 20)
ROWS = 256
CHUNKS = 4
WIDTH = 512


def split(value):
    high = value.astype(BF16)
    return high, (value - high.astype(F32)).astype(BF16)


def dot3(left, right, dims):
    dot = functools.partial(lax.dot_general, dimension_numbers=dims, preferred_element_type=F32)
    return dot(left[0], right[0]) + (dot(left[0], right[1]) + dot(left[1], right[0]))


def swap_into(value, high_ref, low_ref):
    lane = lax.broadcasted_iota(jnp.int32, (16, 128), 1)
    for pair in range(8):
        for tile in range(8):
            first = value[32 * pair : 32 * pair + 16, 128 * tile : 128 * tile + 128]
            second = value[32 * pair + 16 : 32 * pair + 32, 128 * tile : 128 * tile + 128]
            even = jnp.where(lane < 64, first, pltpu.roll(second, 64, 1))
            odd = jnp.where(lane < 64, pltpu.roll(first, 64, 1), second)
            columns = slice(128 * pair, 128 * pair + 128)
            for start, part in ((16 * tile, even), (128 + 16 * tile, odd)):
                high, low = split(part)
                high_ref[start : start + 16, columns] = high
                low_ref[start : start + 16, columns] = low


def unswap_into(value, high_ref, low_ref):
    lane = lax.broadcasted_iota(jnp.int32, (16, 128), 1)
    for pair in range(8):
        for tile in range(8):
            columns = slice(128 * pair, 128 * pair + 128)
            even = value[16 * tile : 16 * tile + 16, columns]
            odd = value[128 + 16 * tile : 128 + 16 * tile + 16, columns]
            first = jnp.where(lane < 64, even, pltpu.roll(odd, 64, 1))
            second = jnp.where(lane < 64, pltpu.roll(even, 64, 1), odd)
            columns = slice(128 * tile, 128 * tile + 128)
            for start, part in ((32 * pair, first), (32 * pair + 16, second)):
                high, low = split(part)
                high_ref[start : start + 16, columns] = high
                low_ref[start : start + 16, columns] = low


def assemble(offsets_ref, piece_refs, whole_ref, sems, high_ref, low_ref):
    block = 64
    copies = []
    count = 0
    for piece in piece_refs:
        for part in range(piece.shape[0] // block):
            start = pl.multiple_of(offsets_ref[count], block)
            target = whole_ref.at[pl.ds(start, block)]
            copies.append((pltpu.make_async_copy(piece.at[pl.ds(part * block, block)], target, sems.at[count]), start))
            count += 1
    for copy, _ in copies:
        copy.start()
    for copy, start in copies:
        copy.wait()

        def some(index, carry, start=start):
            rows = pl.ds(pl.multiple_of(start + index * 16, 16), 16)
            high, low = split(whole_ref[rows, :])
            high_ref[rows, :] = high
            low_ref[rows, :] = low
            return carry

        lax.fori_loop(0, block // 16, some, 0)


def chunk_of(ref):
    return ref.at[pl.ds(pl.multiple_of(pl.program_id(0) * ROWS, ROWS), ROWS)]


def back_kernel(pieces, offsets_ref, *refs):
    piece_refs = refs[:pieces]
    rows_ref, site_ref = refs[pieces : pieces + 2]
    whole_high, whole_low, back_high, back_low, swapped_high, swapped_low, whole, sems = refs[pieces + 2 :]

    @pl.when(pl.program_id(0) == 0)
    def _():
        assemble(offsets_ref, piece_refs, whole, sems, whole_high, whole_low)

    section = dot3(split(rows_ref[...]), (whole_high[...], whole_low[...]), NN)
    swapped_high, swapped_low = chunk_of(swapped_high), chunk_of(swapped_low)
    swap_into(section, swapped_high, swapped_low)
    mixed = dot3(split(site_ref[...]), (swapped_high[...], swapped_low[...]), NN)
    unswap_into(mixed, chunk_of(back_high), chunk_of(back_low))


def block_of(ref):
    return ref.at[pl.ds(pl.multiple_of(pl.program_id(1) * WIDTH, WIDTH), WIDTH)]


def place(terms, sources_ref, staged, ahead_ref, behind_ref, kept_ref):
    for a in range(16):
        staged[:, a, :] = terms[16 * a : 16 * a + 16, :]
    slot = 0
    for ref in (ahead_ref, behind_ref, kept_ref):
        for block in range(ref.shape[0]):
            ref[block] = staged[pl.ds(sources_ref[slot] * 2, 2)]
            slot += 1


def edge_kernel(pieces, offsets_ref, sources_ref, *refs):
    piece_refs = refs[:pieces]
    back_high_ref, back_low_ref = refs[pieces : pieces + 2]
    whole_high, whole_low, ahead_ref, behind_ref, kept_ref, whole, staged, sems = refs[pieces + 2 :]

    @pl.when((pl.program_id(0) == 0) & (pl.program_id(1) == 0))
    def _():
        assemble(offsets_ref, piece_refs, whole, sems, whole_high, whole_low)

    rows = chunk_of(back_high_ref)[...], chunk_of(back_low_ref)[...]
    terms = dot3(rows, (block_of(whole_high)[...], block_of(whole_low)[...]), NT)
    place(terms, sources_ref, staged, ahead_ref, behind_ref, kept_ref)


def first_kernel(
    edge_ref,
    right_high_ref,
    right_low_ref,
    site_matrix_ref,
    swapped_high_ref,
    swapped_low_ref,
    second_high_ref,
    second_low_ref,
    site_ref,
    first_high,
    first_low,
):
    first = dot3(split(edge_ref[...]), (right_high_ref[...], right_low_ref[...]), NN)
    swap_into(first, first_high, first_low)
    mixed = dot3(split(site_matrix_ref[...]), (first_high[...], first_low[...]), TN)
    unswap_into(mixed, chunk_of(second_high_ref), chunk_of(second_low_ref))
    swapped = chunk_of(swapped_high_ref)[...], chunk_of(swapped_low_ref)[...]
    site = dot3((first_high[...], first_low[...]), swapped, NT)

    @pl.when(pl.program_id(0) == 0)
    def _():
        site_ref[...] = site

    @pl.when(pl.program_id(0) > 0)
    def _():
        site_ref[...] += site


def left_kernel(
    sources_ref, second_high_ref, second_low_ref, high_ref, low_ref, ahead_ref, behind_ref, kept_ref, staged
):
    rows = chunk_of(second_high_ref)[...], chunk_of(second_low_ref)[...]
    terms = dot3(rows, (block_of(high_ref)[...], block_of(low_ref)[...]), NT)
    place(terms, sources_ref, staged, ahead_ref, behind_ref, kept_ref)


def right_kernel(places_ref, back_high_ref, back_low_ref, edge_ref, own_ref, other_ref, turned_high, turned_low, placed):
    @pl.when(pl.program_id(0) == 0)
    def _():
        def turn(chunk, carry):
            rows = pl.ds(pl.multiple_of(chunk * ROWS, ROWS), ROWS)
            turned_high[:, rows] = back_high_ref[rows, :].T
            turned_low[:, rows] = back_low_ref[rows, :].T
            return carry

        lax.fori_loop(0, CHUNKS, turn, 0)

    terms = dot3((turned_high[...], turned_low[...]), split(edge_ref[...]), NN)
    for block in range(16):
        start = pl.multiple_of(places_ref[block], 64)
        placed[pl.ds(start, 64), :] = terms[64 * block : 64 * block + 64, :]
    own_ref[...] = placed[:512, :]
    other_ref[...] = placed[512:, :]


def resident(shape):
    return pl.BlockSpec(shape, lambda *_: (0,) * len(shape))


OUTSIDE = pl.BlockSpec(memory_space=pltpu.HBM)
HELD = pl.BlockSpec(memory_space=pltpu.VMEM)
SQUARE = jax.ShapeDtypeStruct((1024, 1024), BF16)
CHUNK = pl.BlockSpec((ROWS, 1024), lambda i, *_: (i, 0))


def back_call(offsets, pieces, rows, site_matrix):
    return pl.pallas_call(
        functools.partial(back_kernel, len(pieces)),
        out_shape=(SQUARE,) * 6,
        grid_spec=pltpu.PrefetchScalarGridSpec(
            num_scalar_prefetch=1,
            grid=(CHUNKS,),
            in_specs=[OUTSIDE] * len(pieces) + [CHUNK, resident((256, 256))],
            out_specs=[HELD] * 6,
            scratch_shapes=[pltpu.VMEM((1024, 1024), F32), pltpu.SemaphoreType.DMA((16,))],
        ),
        compiler_params=PARAMS,
        name="back",
    )(offsets, *pieces, rows, site_matrix)


BLOCKS = tuple(jax.ShapeDtypeStruct((count, 2, 64, 1024), F32) for count in (2, 2, 4))
BLOCK_SPECS = [pl.BlockSpec((count, 2, 16, WIDTH), lambda i, j, *_: (0, 0, i, j)) for count in (2, 2, 4)]


def edge_call(offsets, sources, pieces, back_split):
    return pl.pallas_call(
        functools.partial(edge_kernel, len(pieces)),
        out_shape=(SQUARE, SQUARE, *BLOCKS),
        grid_spec=pltpu.PrefetchScalarGridSpec(
            num_scalar_prefetch=2,
            grid=(CHUNKS, 1024 // WIDTH),
            in_specs=[OUTSIDE] * len(pieces) + [HELD, HELD],
            out_specs=[HELD] * 2 + BLOCK_SPECS,
            scratch_shapes=[
                pltpu.VMEM((1024, 1024), F32),
                pltpu.VMEM((16, 16, WIDTH), F32),
                pltpu.SemaphoreType.DMA((16,)),
            ],
        ),
        compiler_params=PARAMS,
        name="edge",
    )(offsets, sources, *pieces, *back_split)


def first_call(edge_rows, right_split, site_matrix, swapped_split):
    return pl.pallas_call(
        first_kernel,
        out_shape=(SQUARE, SQUARE, jax.ShapeDtypeStruct((256, 256), F32)),
        grid=(CHUNKS,),
        in_specs=[CHUNK] + [HELD] * 2 + [resident((256, 256))] + [HELD] * 2,
        out_specs=[HELD, HELD, resident((256, 256))],
        scratch_shapes=[pltpu.VMEM((ROWS, 1024), BF16)] * 2,
        compiler_params=PARAMS,
        name="first",
    )(edge_rows, *right_split, site_matrix, *swapped_split)


def left_call(sources, second_split, cotangent_split):
    return pl.pallas_call(
        left_kernel,
        out_shape=BLOCKS,
        grid_spec=pltpu.PrefetchScalarGridSpec(
            num_scalar_prefetch=1,
            grid=(CHUNKS, 1024 // WIDTH),
            in_specs=[HELD] * 4,
            out_specs=BLOCK_SPECS,
            scratch_shapes=[pltpu.VMEM((16, 16, WIDTH), F32)],
        ),
        compiler_params=PARAMS,
        name="left",
    )(sources, *second_split, *cotangent_split)


def right_call(places, back_split, edge_rows):
    column = lambda rows: pl.BlockSpec((rows, 256), lambda i, *_: (0, i))
    return pl.pallas_call(
        right_kernel,
        out_shape=(jax.ShapeDtypeStruct((512, 1024), F32),) * 2,
        grid_spec=pltpu.PrefetchScalarGridSpec(
            num_scalar_prefetch=1,
            grid=(4,),
            in_specs=[HELD] * 2 + [column(1024)],
            out_specs=[column(512)] * 2,
            scratch_shapes=[pltpu.VMEM((1024, 1024), BF16)] * 2 + [pltpu.VMEM((1024, 256), F32)],
        ),
        compiler_params=PARAMS,
        name="right",
    )(places, *back_split, edge_rows)


def row_permute(value, z, y, core):
    pairs = []
    for source in range(16):
        there = ((source // 8) ^ z) * 8 + ((source // 2 + y) % 4) * 2 + ((source % 2) ^ core)
        pairs.append((source, there))
    return lax.ppermute(value, "row", pairs)


def col_permute(value, z, x):
    return lax.ppermute(value, "col", [(i, ((i // 4) ^ z) * 4 + (i + x) % 4) for i in range(8)])


def col_reduce(ahead, behind, kept):
    from_behind = col_permute(ahead, 0, 1)
    from_ahead = col_permute(behind, 0, 3)
    sums = kept[0] + from_behind[0], kept[1] + from_ahead[0]
    far_behind = col_permute(sums[0], 0, 1)
    far_ahead = col_permute(sums[1], 0, 3)
    other = kept[3] + from_behind[1] + far_ahead
    same = kept[2] + from_ahead[1] + far_behind
    last = col_permute(other, 1, 0)
    return jnp.transpose(same + last, (1, 0, 2))


def dense(value):
    cols, bond, width = value.shape
    return jnp.transpose(value.reshape(cols, 2, 8, width), (3, 2, 1, 0)).reshape(width, bond * cols)


def take(value, index):
    return lax.dynamic_index_in_dim(value, index, 0, keepdims=False, allow_negative_indices=False)


def on_device(edge_tensor, site_tensor, left_isometry, right_isometry, cotangent):
    row = lax.axis_index("row").astype(jnp.int32)
    col = lax.axis_index("col").astype(jnp.int32)
    z, y, core = row >> 3, (row >> 1) & 3, row & 1
    edge_rows = edge_tensor.reshape(1024, 1024)
    left_rows = pltpu.with_memory_space_constraint(left_isometry.reshape(1024, 1024), pltpu.HBM)

    def offset_of(other_z, steps, other_core):
        other_z, steps, other_core = (np.array(list(v), np.int32) for v in (other_z, steps, other_core))
        return ((z ^ other_z) * 8 + ((y - steps) & 3) * 2 + (core ^ other_core)) * 64

    site_matrix = jnp.transpose(site_tensor, (2, 1, 3, 0)).reshape(256, 256)
    order = [(j, steps, c) for c in (0, 1) for j in (0, 1) for steps in (0, 1, 3, 2)]
    cotangent_offsets = offset_of(*zip(*order))
    order = [(j, steps, c) for c in (0, 1) for steps in (0, 1, 3, 2) for j in (0, 1)]
    isometry_offsets = offset_of(*zip(*order))
    steps = np.array([2, 1, 2, 3, 1, 3, 0, 0], np.int32)
    others = np.array([0, 1, 1, 0, 0, 1, 0, 1], np.int32)
    sources = ((col >> 2) ^ others) * 4 + ((col + steps) & 3)
    blocks = np.array([(i % 2) * 8 + i // 2 for i in range(16)], np.int32)
    places = (((blocks & 1) ^ core) * 8 + (((blocks >> 1) - y) & 3) * 2 + ((blocks >> 3) ^ z)) * 64
    cores, sides = [core, core ^ 1], [z, z ^ 1]
    ahead = [(y + k) & 3 for k in range(4)]
    first_row, at_low_z, at_low_core = ((4 - y) & 3) * 32, z == 0, core == 0

    early = dense(cotangent)
    early, right_isometry = lax.optimization_barrier((early, right_isometry))
    other = row_permute(early, 1, 0, 0)
    nearest = [row_permute(early, 0, steps, 0) for steps in (1, 3, 2)]
    values = (cotangent_offsets, isometry_offsets, sources, places)
    indices = (*cores, *sides, *ahead, first_row, at_low_z, at_low_core)
    other, values, indices = lax.optimization_barrier((other, values, indices))
    cotangent_offsets, isometry_offsets, sources, places = values
    cores, sides, ahead, (first_row, at_low_z, at_low_core) = indices[:2], indices[2:4], indices[4:8], indices[8:]
    own = dense(right_isometry)
    pair = jnp.concatenate([own, row_permute(own, 1, 0, 0)], 0)
    pieces = [early, *nearest, other, *(row_permute(other, 0, steps, 0) for steps in (1, 3, 2))]
    pairs = [pair] + [row_permute(pair, 0, steps, 0) for steps in (1, 3, 2)]

    pieces[3], site_matrix = lax.optimization_barrier((pieces[3], site_matrix))
    pieces += [row_permute(piece, 0, 0, 1) for piece in pieces]
    cotangent_high, cotangent_low, *rest = back_call(cotangent_offsets, pieces, left_rows, site_matrix)
    back_split, swapped_split = rest[:2], rest[2:]

    pairs += [row_permute(piece, 0, 0, 1) for piece in pairs]
    right_high, right_low, *edge_terms = edge_call(isometry_offsets, sources, pairs, back_split)
    edge_gradient = col_reduce(*edge_terms)
    *second_split, site_terms = first_call(edge_rows, (right_high, right_low), site_matrix, swapped_split)
    left_terms = left_call(sources, second_split, (cotangent_high, cotangent_low))
    left_gradient = col_reduce(*left_terms)

    right_own, right_other = right_call(places, back_split, edge_rows)

    part = site_terms.reshape(2, 4, 2, 16, 256)

    def corner(k):
        start = (cores[k >> 1], 0, sides[k & 1], 0, 0)
        return lax.dynamic_slice(part, start, (1, 4, 1, 16, 256), allow_negative_indices=False).reshape(64, 256)

    part = corner(0) + sum(row_permute(corner(k), k & 1, 0, k >> 1) for k in (1, 2, 3))
    part = part.reshape(4, 16, 256)
    sends = [row_permute(take(part, ahead[k]), 0, k, 0) for k in (1, 2, 3)]
    part = take(part, ahead[0]) + sum(sends)
    part = part + col_permute(part, 1, 0)
    part = part + sum(col_permute(part, 0, k) for k in (1, 2, 3))
    other = row_permute(part, 1, 0, 0)
    part = jnp.where(at_low_z, jnp.concatenate([part, other], 0), jnp.concatenate([other, part], 0))
    ring = [part] + [row_permute(part, 0, k, 0) for k in (3, 2, 1)]
    ring = jnp.concatenate(ring + ring, 0)
    part = lax.dynamic_slice(ring, (first_row, 0), (128, 256), allow_negative_indices=False)
    other = row_permute(part, 0, 0, 1)
    part = jnp.where(at_low_core, jnp.concatenate([part, other], 0), jnp.concatenate([other, part], 0))
    site_gradient = jnp.transpose(part.reshape(16, 16, 16, 16), (3, 1, 0, 2))

    right_own = right_own.reshape(4, 2, 64, 1024)
    received = row_permute(right_other, 0, 0, 1).reshape(4, 2, 64, 1024)
    total = [right_own[k] + received[k] for k in range(4)]
    total = total[0] + sum(row_permute(total[k], 0, k, 0) for k in (1, 3, 2))
    right_gradient = total[0] + row_permute(total[1], 1, 0, 0)

    return (
        edge_gradient,
        site_gradient,
        left_gradient,
        right_gradient.reshape(64, 1, 1024),
    )


def solution(mesh):
    in_specs = (
        P("row", None, None),
        P(),
        P("row", None, None),
        P("col", None, "row"),
        P("col", None, "row"),
    )
    out_specs = (P("row", "col", None), P(), P("row", "col", None), P("col", "row", None))

    return jax.shard_map(on_device, mesh=mesh, in_specs=in_specs, out_specs=out_specs, check_vma=False)
```
